768 devices in a mesh: axial: 48 (over z_lo, y, core), radial: 16 (over z_hi, x).
Axes of the slice: x: 4, y: 8, z: 12 (z_hi: 4, z_lo: 3; z = z_hi * 3 + z_lo), core: 2. Of those that a mesh axis runs over, the one named last changes fastest.
Arguments:
- species: float32 [5, 384, 128, 128], P(None, 'axial', 'radial')
- velocity: float32 [3, 384, 128, 128], P(None, 'axial', 'radial'), may hold values from -4 to 4
- diffusivity: float32 [384, 128, 128], P('axial', 'radial'), may hold values from 0.3 to 1
- parcels: float32 [48, 16, 16, 2048], P('axial', 'radial')
- counts: int32 [48, 16], P('axial', 'radial'), may hold values from 256 to 2048, as said below
- cells: int32 [48, 16, 2048], P('axial', 'radial'), may hold values from 0 to 8191, as said below
- leave_slots: int32 [48, 16, 4, 64], P('axial', 'radial'), may hold values from 0 to 2047, as said below
- leave_counts: int32 [48, 16, 4], P('axial', 'radial'), may hold values from 16 to 64, as said below
Outputs:
- species_out: float32 [5, 384, 128, 128], P(None, 'axial', 'radial')
- velocity_out: float32 [3, 384, 128, 128], P(None, 'axial', 'radial')
- staying: float32 [48, 16, 16, 2048], P('axial', 'radial')
- arrivals: float32 [48, 16, 4, 16, 64], P('axial', 'radial')
The draws below stay inside these ranges and needn't reach their ends.
Inputs may be any that keep to these rules, and one draw needn't show every extreme that they name: `counts`: block 0 along the first dimension, 8 along the second is full; blocks near the injector hold several times the mean. `cells`: Non-decreasing along the slots of a block; slots that are not live hold 8191. `leave_slots`: entries below a face's count are live slots of that block, all distinct over the four faces; entries at or beyond the count are 0. `leave_counts`: some block sends 64 parcels through each of its faces.
All inputs are finite; a program needn't handle non-finite values.
Results may differ from the reference program's by a relative error of at most 0.0003.
Values sent between devices are 32-bit elements; how exact they have to be, the bound alone decides.
A program may use at most 32 MiB of HBM per device.

```python
import math
import jax
import jax.numpy as jnp

CX = 8
CY = 8
CZ = 128
PCAP = 2048
MCAP = 64
CELLS = 8192
SLABS = 48
COLUMNS = 16
NX = 384
NY = 128
NZ = 128


def block_counts(key):
    slab_ids = jnp.arange(SLABS, dtype=jnp.int32)[:, None]
    column_ids = jnp.arange(COLUMNS, dtype=jnp.int32)[None, :]
    drawn = jax.random.randint(jax.random.fold_in(key, 1), (SLABS, COLUMNS), PCAP // 8, PCAP // 4 + 1)
    crowded = PCAP - jax.random.randint(jax.random.fold_in(key, 2), (SLABS, COLUMNS), 0, PCAP // 4 + 1)
    cone = (slab_ids < max(1, SLABS // 4)) & ((column_ids == COLUMNS // 2) | (column_ids == COLUMNS // 2 - 1))
    loads = jnp.where(cone, crowded, drawn)
    return jnp.where((slab_ids == 0) & (column_ids == COLUMNS // 2), PCAP, loads).astype(jnp.int32)


def face_loads(key):
    loads = jax.random.randint(jax.random.fold_in(key, 303), (SLABS, COLUMNS, 4), MCAP // 4, MCAP + 1)
    slab_ids = jnp.arange(SLABS, dtype=jnp.int32)[:, None, None]
    column_ids = jnp.arange(COLUMNS, dtype=jnp.int32)[None, :, None]
    busiest = (slab_ids == 0) & (column_ids == COLUMNS // 2)
    return jnp.where(busiest, MCAP, loads).astype(jnp.int32)


def draw_counts(key, part):
    return block_counts(jax.random.fold_in(key, 101))


def draw_cells(key, part):
    loads = block_counts(jax.random.fold_in(key, 101))
    raw_cells = jax.random.randint(jax.random.fold_in(key, 202), (SLABS, COLUMNS, PCAP), 0, CELLS)
    slot_ids = jnp.arange(PCAP, dtype=jnp.int32)
    raw_cells = jnp.where(slot_ids[None, None, :] < loads[:, :, None], raw_cells, CELLS - 1)
    return jnp.sort(raw_cells, axis=-1).astype(jnp.int32)


def draw_leave_counts(key, part):
    return face_loads(key)


def draw_leave_slots(key, part):
    loads = block_counts(jax.random.fold_in(key, 101))
    faces = face_loads(key)
    slot_ids = jnp.arange(PCAP, dtype=jnp.int32)
    scores = jax.random.randint(jax.random.fold_in(key, 404), (SLABS, COLUMNS, PCAP), 0, 16384) * PCAP + slot_ids[None, None, :]
    scores = scores + jnp.where(slot_ids[None, None, :] >= loads[:, :, None], 2 ** 28, 0)
    last_full = (slot_ids[None, None, :] == PCAP - 1) & (loads[:, :, None] == PCAP)
    scores = scores - jnp.where(last_full, 2 ** 28, 0)
    order = jnp.argsort(scores, axis=-1)[:, :, :4 * MCAP].reshape(SLABS, COLUMNS, 4, MCAP).astype(jnp.int32)
    keep = jnp.arange(MCAP, dtype=jnp.int32)[None, None, None, :] < faces[:, :, :, None]
    return jnp.where(keep, order, 0).astype(jnp.int32)


def draw_parcels(key, part):
    shape = (SLABS, COLUMNS, 16, PCAP)
    normal_values = jax.random.normal(jax.random.fold_in(key, 505), shape, jnp.float32)
    level = jax.random.uniform(jax.random.fold_in(key, 606), shape, jnp.float32)
    row_ids = jnp.arange(16, dtype=jnp.int32)[None, None, :, None]
    mass = jnp.exp(math.log(0.5) + level * math.log(4.0))
    response = jnp.exp(math.log(0.5) + level * math.log(10.0))
    evaporation = jnp.exp(math.log(0.3) + level * math.log(2.0 / 0.3))
    values = jnp.where(row_ids == 3, mass, jnp.where(row_ids == 4, response, jnp.where(row_ids == 5, evaporation, normal_values)))
    return values.astype(jnp.float32)


def draw_species(key, part):
    shape = (5, NX, NY, NZ)
    return (1.0 + 0.5 * jax.random.normal(jax.random.fold_in(key, 808), shape, jnp.float32)).astype(jnp.float32)


def level_of(own_key, shape, cuts, least, largest):
    level = 1.0
    for dim, shards_of in cuts:
        steps = jax.random.uniform(jax.random.fold_in(jax.random.fold_in(own_key, 6), dim), (shards_of,), jnp.float32, least / len(cuts), largest / len(cuts))
        level = level * jnp.repeat(jnp.exp(steps), shape[dim] // shards_of).reshape((-1,) + (1,) * (len(shape) - 1 - dim))
    return level


def noise(key, dims, spread, bound, split=(), held_as=jnp.bfloat16):
    array = spread * jax.random.normal(key, dims, jnp.float32)
    if split:
        array = array * level_of(key, dims, split, -0.22, 0.18)
    return jnp.clip(array, -bound, bound).astype(held_as)


def setup_inputs(seed: int = 0) -> dict:
    arg_keys = jax.random.split(jax.random.key(seed), 9)
    species = draw_species(jax.random.fold_in(arg_keys[8], 71), 0)
    velocity = noise(arg_keys[1], (3, NX, NY, NZ), 1.0, 4.0, ((1, 48), (2, 16)), jnp.float32)
    diffusivity = jnp.clip(jnp.exp(math.log(1.0) - 1.2039728 * jax.random.uniform(arg_keys[2], (NX, NY, NZ), jnp.float32) ** level_of(arg_keys[2], (NX, NY, NZ), ((0, 48), (1, 16)), -0.2, 0.2)), 0.3, 1.0)
    parcels = draw_parcels(jax.random.fold_in(arg_keys[8], 71), 0)
    counts = draw_counts(jax.random.fold_in(arg_keys[8], 71), 0)
    cells = draw_cells(jax.random.fold_in(arg_keys[8], 71), 0)
    leave_slots = draw_leave_slots(jax.random.fold_in(arg_keys[8], 71), 0)
    leave_counts = draw_leave_counts(jax.random.fold_in(arg_keys[8], 71), 0)
    return {"species": species, "velocity": velocity, "diffusivity": diffusivity, "parcels": parcels, "counts": counts, "cells": cells, "leave_slots": leave_slots, "leave_counts": leave_counts}


time_step = 0.1


def coefficient(vel_first, vel_second, vel_third, base_rate):
    kinetic = vel_first * vel_first + vel_second * vel_second + vel_third * vel_third
    return base_rate * (1.0 + 0.5 * jnp.tanh(0.5 * kinetic))


def operate(values, diffusion):
    widths = [(0, 0)] * (values.ndim - 1) + [(1, 1)]
    padded = jnp.pad(values, widths)
    diffusion_padded = jnp.pad(diffusion, ((0, 0), (0, 0), (1, 1)))
    weight_first = 0.5 * (diffusion[1:] + diffusion[:-1])
    flux_first = weight_first * (values[..., 1:, :, :] - values[..., :-1, :, :])
    change_first = flux_first[..., 1:, :, :] - flux_first[..., :-1, :, :]
    weight_second = 0.5 * (diffusion[:, 1:] + diffusion[:, :-1])
    flux_second = weight_second * (values[..., :, 1:, :] - values[..., :, :-1, :])
    change_second = flux_second[..., :, 1:, :] - flux_second[..., :, :-1, :]
    weight_third = 0.5 * (diffusion_padded[:, :, 1:] + diffusion_padded[:, :, :-1])
    flux_third = weight_third * (padded[..., 1:] - padded[..., :-1])
    change_third = flux_third[..., 1:] - flux_third[..., :-1]
    return change_first[..., :, 1:-1, :] + change_second[..., 1:-1, :, :] + change_third[..., 1:-1, 1:-1, :]


def advance_parcels(parcel_block, live_count, cell_index, slot_table, face_counts, gas_flat):
    slots_total = parcel_block.shape[-1]
    movers = slot_table.shape[-1]
    gas_here = jnp.take(gas_flat, cell_index, axis=1)
    old_velocity = parcel_block[0:3]
    old_mass = parcel_block[3]
    response = parcel_block[4]
    evaporation = parcel_block[5]
    drag_force = response * (gas_here - old_velocity)
    new_velocity = old_velocity + time_step * drag_force
    new_mass = old_mass * (1.0 - time_step * evaporation)
    new_position = parcel_block[6:9] + time_step * new_velocity
    pushed = jnp.concatenate([new_velocity, new_mass[None], parcel_block[4:6], new_position, parcel_block[9:]], axis=0)
    slot_ids = jnp.arange(slots_total, dtype=jnp.int32)
    live_weight = (slot_ids < live_count).astype(jnp.float32)
    deposits = jnp.stack([old_mass * evaporation, -old_mass * drag_force[0], -old_mass * drag_force[1], -old_mass * drag_force[2]], axis=0) * live_weight[None, :]
    source = jnp.zeros((4, gas_flat.shape[1]), jnp.float32).at[:, cell_index].add(deposits)
    face_valid = (jnp.arange(movers, dtype=jnp.int32)[None, :] < face_counts[:, None]).astype(jnp.float32)
    leaving = jnp.zeros((slots_total,), jnp.float32).at[slot_table.reshape(-1)].max(face_valid.reshape(-1))
    staying = pushed * (live_weight * (1.0 - leaving))[None, :]
    outgoing = jnp.transpose(jnp.take(pushed, slot_table, axis=1), (1, 0, 2)) * face_valid[:, None, :]
    return staying, outgoing, source


def pad_plane(values):
    return jnp.pad(values, ((1, 1), (1, 1), (0, 0)))


def reference(species, velocity, diffusivity, parcels, counts, cells, leave_slots, leave_counts):
    gas_blocks = velocity.reshape(3, SLABS, CX, COLUMNS, CY, CZ).transpose(1, 3, 0, 2, 4, 5).reshape(SLABS, COLUMNS, 3, CELLS)
    staying, outgoing, source = jax.vmap(jax.vmap(advance_parcels))(parcels, counts, cells, leave_slots, leave_counts, gas_blocks)
    source_grid = source.reshape(SLABS, COLUMNS, 4, CX, CY, CZ).transpose(2, 0, 3, 1, 4, 5).reshape(4, NX, NY, NZ)
    base_padded = pad_plane(diffusivity)
    start = coefficient(pad_plane(velocity[0]), pad_plane(velocity[1]), pad_plane(velocity[2]), base_padded)
    fields_in = [species[member] for member in range(5)] + [velocity[member] for member in range(3)]
    first = [fields_in[member] + time_step * operate(pad_plane(fields_in[member]), start) for member in range(8)]
    later = coefficient(pad_plane(first[5]), pad_plane(first[6]), pad_plane(first[7]), base_padded)
    second = [0.5 * (fields_in[member] + first[member] + time_step * operate(pad_plane(first[member]), later)) for member in range(8)]
    zero_grid = jnp.zeros((NX, NY, NZ), jnp.float32)
    added = [source_grid[0], zero_grid, zero_grid, zero_grid, zero_grid, source_grid[1], source_grid[2], source_grid[3]]
    result = [second[member] + time_step * added[member] for member in range(8)]
    species_out = jnp.stack(result[:5], axis=0)
    velocity_out = jnp.stack(result[5:], axis=0)
    zero_slab = jnp.zeros_like(outgoing[:1, :, 0])
    from_below = jnp.concatenate([zero_slab, outgoing[:-1, :, 0]], axis=0)
    from_above = jnp.concatenate([outgoing[1:, :, 1], zero_slab], axis=0)
    zero_column = jnp.zeros_like(outgoing[:, :1, 2])
    from_left = jnp.concatenate([zero_column, outgoing[:, :-1, 2]], axis=1)
    from_right = jnp.concatenate([outgoing[:, 1:, 3], zero_column], axis=1)
    arrivals = jnp.stack([from_below, from_above, from_left, from_right], axis=2)
    return (species_out, velocity_out, staying, arrivals)
```

```python
import functools

import jax
import jax.numpy as jnp
from jax import lax
from jax.experimental import pallas as pl
from jax.experimental.pallas import tpu as pltpu
from jax.sharding import PartitionSpec as P

MESH = pl.DeviceIdType.MESH
F32, BF16, I32 = jnp.float32, jnp.bfloat16, jnp.int32
time_step = 0.1
CHUNK = 512
STEPS = ((0, 1), (0, -1), (1, 0), (-1, 0), (1, 1), (1, -1), (-1, 1), (-1, -1))
FACES = ((1, 0), (-1, 0), (0, 1), (0, -1))


def ranges(step, depth):
    if step == 0:
        return (2, 8), (2, 8)
    if step > 0:
        return (10 - depth, depth), (2 - depth, depth)
    return (2, depth), (10, depth)


def coefficient(values, base):
    row = lax.broadcasted_iota(I32, (8, 128), 0)
    kinetic = jnp.where(row >= 5, values * values, 0.0)
    for shift in (4, 2, 1):
        kinetic = kinetic + pltpu.roll(kinetic, shift, 0)
    return base * (1.0 + 0.5 * jnp.tanh(0.5 * kinetic))


def pieces(x):
    high = x.astype(BF16)
    rest = x - high.astype(F32)
    middle = rest.astype(BF16)
    low = (rest - middle.astype(F32)).astype(BF16)
    return high, middle, low


def one_hot(rows, index):
    row = lax.broadcasted_iota(I32, (rows, index.shape[1]), 0)
    return jnp.where(row == index, 1.0, 0.0).astype(BF16)


def dot_nt(a, b):
    return lax.dot_general(a, b, (((1,), (1,)), ((), ())), preferred_element_type=F32)


def exchange_kernel(
    n_a, n_r, species, velocity, diffusivity, parcels, counts, cells, slots, faces,
    ext, base, start, source, staying, arrivals,
    vel, par, cnt, cel, slo, fac, vel3, pushed, leaving, outgoing,
    load_sem, send_sem, recv_sem, base_send, base_recv, row_send, row_recv,
):
    a, r = lax.axis_index("axial"), lax.axis_index("radial")

    def there(step_a, step_r):
        ok = None
        for step, at, size in ((step_a, a, n_a), (step_r, r, n_r)):
            if step:
                here = at < size - 1 if step > 0 else at > 0
                ok = here if ok is None else jnp.logical_and(ok, here)
        return ok

    barrier = pltpu.get_barrier_semaphore()
    total = jnp.int32(0)
    for da, dr in STEPS:
        ok = there(da, dr)
        total = total + ok.astype(I32)

        @pl.when(ok)
        def _(da=da, dr=dr):
            pl.semaphore_signal(barrier, inc=1, device_id=(a + da, r + dr), device_id_type=MESH)

    loads = [pltpu.make_async_copy(species.at[f], ext.at[2:10, 2:10, f], load_sem.at[f]) for f in range(5)]
    loads += [pltpu.make_async_copy(velocity.at[k], ext.at[2:10, 2:10, 5 + k], load_sem.at[5 + k]) for k in range(3)]
    loads.append(pltpu.make_async_copy(diffusivity, base.at[2:10, 2:10, 0], load_sem.at[8]))
    own_loads = len(loads)
    for k, (src, dst) in enumerate(
        ((velocity, vel), (parcels, par), (counts, cnt), (cells, cel), (slots, slo), (faces, fac))
    ):
        loads.append(pltpu.make_async_copy(src, dst, load_sem.at[9 + k]))
    for load in loads:
        load.start()

    zero2 = jnp.zeros((2, 8, 8, 128), F32)
    zero3 = jnp.zeros((8, 2, 8, 128), F32)
    corner = jnp.zeros((8, 128), F32)

    def clear_corner(x, y):
        ext[x, y] = corner
        base[x, y] = corner[:1]

    @pl.when(a == 0)
    def _():
        ext[0:2, 2:10] = zero2
        base[0:2, 2:10] = zero2[:, :, :1]
        arrivals[0] = jnp.zeros((16, 64), F32)
        clear_corner(1, 1)
        clear_corner(1, 10)

    @pl.when(a == n_a - 1)
    def _():
        ext[10:12, 2:10] = zero2
        base[10:12, 2:10] = zero2[:, :, :1]
        arrivals[1] = jnp.zeros((16, 64), F32)
        clear_corner(10, 1)
        clear_corner(10, 10)

    @pl.when(r == 0)
    def _():
        ext[2:10, 0:2] = zero3
        base[2:10, 0:2] = zero3[:, :, :1]
        arrivals[2] = jnp.zeros((16, 64), F32)
        clear_corner(1, 1)
        clear_corner(10, 1)

    @pl.when(r == n_r - 1)
    def _():
        ext[2:10, 10:12] = zero3
        base[2:10, 10:12] = zero3[:, :, :1]
        arrivals[3] = jnp.zeros((16, 64), F32)
        clear_corner(1, 10)
        clear_corner(10, 10)

    for load in loads[:own_loads]:
        load.wait()
    pl.semaphore_wait(barrier, total)

    def halo(k):
        da, dr = STEPS[k]
        depth = 1 if da and dr else 2
        (sx, nx), (tx, _) = ranges(da, depth)
        (sy, ny), (ty, _) = ranges(dr, depth)
        device = (a + da, r + dr)
        return (
            pltpu.make_async_remote_copy(
                src_ref=ext.at[sx : sx + nx, sy : sy + ny],
                dst_ref=ext.at[tx : tx + nx, ty : ty + ny],
                send_sem=send_sem.at[k], recv_sem=recv_sem.at[k],
                device_id=device, device_id_type=MESH,
            ),
            pltpu.make_async_remote_copy(
                src_ref=base.at[sx : sx + nx, sy : sy + ny],
                dst_ref=base.at[tx : tx + nx, ty : ty + ny],
                send_sem=base_send.at[k], recv_sem=base_recv.at[k],
                device_id=device, device_id_type=MESH,
            ),
        )

    for k, (da, dr) in enumerate(STEPS):

        @pl.when(there(da, dr))
        def _(k=k):
            for copy in halo(k):
                copy.start()

    for load in loads[own_loads:]:
        load.wait()

    leave_sum = jnp.zeros((16, 128), F32)
    low_hot, high_row = [], []
    for f in range(4):
        member = lax.broadcasted_iota(I32, (1, 64), 1)
        slot = jnp.where(member < fac[0:1, f : f + 1], slo[f : f + 1, :], -1)
        high_row.append(slot >> 7)
        low_hot.append(one_hot(128, slot & 127))
        leave_sum = leave_sum + dot_nt(one_hot(16, slot >> 7), low_hot[f])
    leaving[...] = leave_sum

    vel3[...] = jnp.concatenate(pieces(vel[...].reshape(192, 128)), axis=1)
    source[...] = jnp.zeros((512, 128), F32)

    def parcel_step(c, _):
        span = pl.ds(pl.multiple_of(c * CHUNK, CHUNK), CHUNK)
        cell = cel[:, span]
        plane, depth = cell >> 7, cell & 127
        depth_hot = one_hot(128, depth)
        rows = jnp.dot(vel3[...], jnp.concatenate([depth_hot] * 3, axis=0), preferred_element_type=F32)
        here = lax.broadcasted_iota(I32, (64, CHUNK), 0) == plane
        gas = jnp.concatenate(
            [
                jnp.sum(jnp.where(here, rows[64 * k : 64 * k + 64], 0.0), axis=0, keepdims=True)
                for k in range(3)
            ],
            axis=0,
        )
        old = par[:, span]
        mass, evaporation = old[3:4], old[5:6]
        drag = old[4:5] * (gas - old[0:3])
        new_velocity = old[0:3] + time_step * drag
        pushed[:, span] = old
        pushed[0:3, span] = new_velocity
        pushed[3:4, span] = mass * (1.0 - time_step * evaporation)
        pushed[6:9, span] = old[6:9] + time_step * new_velocity
        live = lax.broadcasted_iota(I32, (1, CHUNK), 1) + c * CHUNK < cnt[0:1, 0:1]
        leave = jnp.concatenate(
            [leaving[pl.ds(c * (CHUNK // 128) + j, 1), :] for j in range(CHUNK // 128)], axis=1
        )
        keep = jnp.logical_and(live, leave == 0.0)
        staying[:, span] = jnp.where(keep, pushed[:, span], 0.0)
        deposit = [mass * evaporation] + [-mass * drag[k : k + 1] for k in range(3)]
        split = [pieces(jnp.where(live, d, 0.0)) for d in deposit]
        added = jnp.zeros((256, 128), F32)
        for p in range(3):
            spread = jnp.concatenate(
                [jnp.where(here, split[k][p].astype(F32), 0.0).astype(BF16) for k in range(4)], axis=0
            )
            added = added + dot_nt(spread, depth_hot)
        source[0:64] += added[0:64]
        source[320:512] += added[64:256]
        return 0

    lax.fori_loop(0, 2048 // CHUNK, parcel_step, 0)

    stacked = jnp.concatenate([pushed[:, 128 * h : 128 * h + 128] for h in range(16)], axis=0)
    stacked3 = jnp.concatenate(pieces(stacked), axis=1)
    for f in range(4):
        picked = jnp.dot(stacked3, jnp.concatenate([low_hot[f]] * 3, axis=0), preferred_element_type=F32)
        out = jnp.zeros((16, 64), F32)
        for h in range(16):
            out = out + jnp.where(high_row[f] == h, picked[16 * h : 16 * h + 16], 0.0)
        outgoing[f] = out

    def own_start(x, _):
        for y in range(2, 10):
            start[x, y] = coefficient(ext[x, y], base[x, y])
        return 0

    lax.fori_loop(2, 10, own_start, 0)

    def row_copy(f):
        da, dr = FACES[f]
        return pltpu.make_async_remote_copy(
            src_ref=outgoing.at[f], dst_ref=arrivals.at[f],
            send_sem=row_send.at[f], recv_sem=row_recv.at[f],
            device_id=(a + da, r + dr), device_id_type=MESH,
        )

    for f in (2, 3, 0, 1):

        @pl.when(there(*FACES[f]))
        def _(f=f):
            row_copy(f).start()

    for k, (da, dr) in enumerate(STEPS):

        @pl.when(there(-da, -dr))
        def _(k=k):
            for copy in halo(k):
                copy.wait_recv()

    for f, (da, dr) in enumerate(FACES):

        @pl.when(there(-da, -dr))
        def _(f=f):
            row_copy(f).wait_recv()

    for k, (da, dr) in enumerate(STEPS):

        @pl.when(there(da, dr))
        def _(k=k):
            for copy in halo(k):
                copy.wait_send()

    for f, (da, dr) in enumerate(FACES):

        @pl.when(there(da, dr))
        def _(f=f):
            row_copy(f).wait_send()


def z_up(x):
    lane = lax.broadcasted_iota(I32, (8, 128), 1)
    return jnp.where(lane == 127, 0.0, pltpu.roll(x, 127, 1))


def change(value, coef, below, below_coef, above, above_coef, flux_y):
    lane = lax.broadcasted_iota(I32, (8, 128), 1)
    flux_x = (coef + above_coef) * (above - value) - (below_coef + coef) * (value - below)
    up = (coef + z_up(coef)) * (z_up(value) - value)
    down = jnp.where(lane == 0, coef * value, pltpu.roll(up, 1, 1))
    return flux_x + flux_y + (up - down)


def stencil_kernel(
    n_a, n_r, ext, base, own_start, source, staying, arrivals,
    species_out, velocity_out, staying_out, arrivals_out,
    start, first, later, result, sems,
):
    a, r = lax.axis_index("axial"), lax.axis_index("radial")
    early = [
        pltpu.make_async_copy(staying, staying_out, sems.at[0]),
        pltpu.make_async_copy(arrivals, arrivals_out, sems.at[1]),
    ]
    for copy in early:
        copy.start()

    def copy_start(x, _):
        for y in range(2, 10):
            start[x, y] = own_start[x, y]
        for y in (0, 1, 10, 11):
            start[x, y] = coefficient(ext[x, y], base[x, y])
        return 0

    lax.fori_loop(2, 10, copy_start, 0)
    for x in (0, 11):
        for y in range(2, 10):
            start[x, y] = coefficient(ext[x, y], base[x, y])
    for x in (1, 10):
        for y in range(1, 11):
            start[x, y] = coefficient(ext[x, y], base[x, y])

    def first_row(x, low, high, outside):
        values = {y: ext[x, y] for y in range(low - 1, high + 1)}
        coefs = {y: start[x, y] for y in range(low - 1, high + 1)}
        fluxes = {y: (coefs[y] + coefs[y + 1]) * (values[y + 1] - values[y]) for y in range(low - 1, high)}
        for y in range(low, high):
            twice = change(
                values[y], coefs[y], ext[x - 1, y], start[x - 1, y], ext[x + 1, y], start[x + 1, y],
                fluxes[y] - fluxes[y - 1],
            )
            new = values[y] + (0.5 * time_step) * twice
            zero = outside
            if y == 1:
                zero = r == 0
            if y == 10:
                zero = r == n_r - 1
            if zero is not None:
                new = jnp.where(zero, 0.0, new)
            first[x, y] = new
            later[x, y] = coefficient(new, base[x, y])

    def inner_row(x, _):
        first_row(x, 1, 11, None)
        return 0

    first_row(1, 2, 10, a == 0)
    first_row(10, 2, 10, a == n_a - 1)
    lax.fori_loop(2, 10, inner_row, 0)

    def second_row(x, _):
        values = {y: first[x, y] for y in range(1, 11)}
        coefs = {y: later[x, y] for y in range(1, 11)}
        fluxes = {y: (coefs[y] + coefs[y + 1]) * (values[y + 1] - values[y]) for y in range(1, 10)}
        for y in range(2, 10):
            twice = change(
                values[y], coefs[y], first[x - 1, y], later[x - 1, y], first[x + 1, y], later[x + 1, y],
                fluxes[y] - fluxes[y - 1],
            )
            cell = (x - 2) * 8 + (y - 2)
            added = source[pl.ds(cell, 8, stride=64), :]
            result[pl.ds(cell, 8, stride=64), :] = (
                0.5 * (ext[x, y] + values[y]) + (0.25 * time_step) * twice + time_step * added
            )
        return 0

    lax.fori_loop(2, 10, second_row, 0)
    last = [
        pltpu.make_async_copy(result.at[0:320], species_out, sems.at[2]),
        pltpu.make_async_copy(result.at[320:512], velocity_out, sems.at[3]),
    ]
    for copy in last:
        copy.start()
    for copy in early + last:
        copy.wait()


def body(n_a, n_r, species, velocity, diffusivity, parcels, counts, cells, leave_slots, leave_counts):
    anywhere = pl.BlockSpec(memory_space=pl.ANY)
    vmem = pl.BlockSpec(memory_space=pltpu.VMEM)
    shape = lambda *dims: jax.ShapeDtypeStruct(dims, F32)
    local = lambda *dims: pltpu.VMEM(dims, F32)
    dma = pltpu.SemaphoreType.DMA
    between = pl.pallas_call(
        functools.partial(exchange_kernel, n_a, n_r),
        name="exchange",
        out_shape=[
            local(12, 12, 8, 128), local(12, 12, 1, 128), local(12, 12, 8, 128), local(512, 128),
            local(16, 2048), local(4, 16, 64),
        ],
        in_specs=[anywhere] * 4 + [pl.BlockSpec(memory_space=pltpu.HBM)] + [anywhere] * 3,
        out_specs=[vmem] * 6,
        scratch_shapes=[
            pltpu.VMEM((3, 8, 8, 128), F32), pltpu.VMEM((16, 2048), F32), pltpu.VMEM((1, 1), I32),
            pltpu.VMEM((1, 2048), I32), pltpu.VMEM((4, 64), I32), pltpu.VMEM((1, 4), I32),
            pltpu.VMEM((192, 384), BF16), pltpu.VMEM((16, 2048), F32), pltpu.VMEM((16, 128), F32),
            pltpu.VMEM((4, 16, 64), F32),
            dma((15,)), dma((8,)), dma((8,)), dma((8,)), dma((8,)), dma((4,)), dma((4,)),
        ],
        compiler_params=pltpu.CompilerParams(collective_id=0, has_side_effects=True),
    )(
        species, velocity, diffusivity, parcels[0, 0], counts, cells[0], leave_slots[0, 0], leave_counts[0],
    )
    species_out, velocity_out, staying, arrivals = pl.pallas_call(
        functools.partial(stencil_kernel, n_a, n_r),
        name="stencil",
        out_shape=[shape(320, 128), shape(192, 128), shape(16, 2048), shape(4, 16, 64)],
        in_specs=[vmem] * 6,
        out_specs=[anywhere] * 4,
        scratch_shapes=[
            pltpu.VMEM((12, 12, 8, 128), F32), pltpu.VMEM((12, 12, 8, 128), F32),
            pltpu.VMEM((12, 12, 8, 128), F32), pltpu.VMEM((512, 128), F32), dma((4,)),
        ],
    )(*[pltpu.with_memory_space_constraint(x, pltpu.VMEM) for x in between])
    return (
        species_out.reshape(5, 8, 8, 128), velocity_out.reshape(3, 8, 8, 128),
        staying[None, None], arrivals[None, None],
    )


def solution(mesh):
    return jax.shard_map(
        functools.partial(body, mesh.shape["axial"], mesh.shape["radial"]),
        mesh=mesh,
        in_specs=(
            P(None, "axial", "radial", None),
            P(None, "axial", "radial", None),
            P("axial", "radial", None),
            P("axial", "radial", None, None),
            P("axial", "radial"),
            P("axial", "radial", None),
            P("axial", "radial", None, None),
            P("axial", "radial", None),
        ),
        out_specs=(
            P(None, "axial", "radial", None),
            P(None, "axial", "radial", None),
            P("axial", "radial", None, None),
            P("axial", "radial", None, None, None),
        ),
        check_vma=False,
    )
```

```python
import functools

import jax
import jax.numpy as jnp
from jax import lax
from jax.experimental import pallas as pl
from jax.experimental.pallas import tpu as pltpu
from jax.sharding import PartitionSpec as P

MESH = pl.DeviceIdType.MESH
F32, BF16, I32 = jnp.float32, jnp.bfloat16, jnp.int32
time_step = 0.1
CHUNK = 512
TRIPS = (
    ((0, 1), (2, 1, 8, 2), (2, 0)), ((0, 1), (9, 1, 8, 2), (9, 0)), ((0, 1), (3, 6, 8, 2), (3, 0)),
    ((0, -1), (2, 1, 2, 2), (2, 10)), ((0, -1), (9, 1, 2, 2), (9, 10)), ((0, -1), (3, 6, 2, 2), (3, 10)),
    ((1, 0), (8, 2, 2, 8), (0, 2)), ((-1, 0), (2, 2, 2, 8), (10, 2)),
    ((1, 0), (9, 1, 1, 1), (1, 1)), ((-1, 0), (2, 1, 1, 1), (10, 1)),
    ((1, 0), (9, 1, 10, 1), (1, 10)), ((-1, 0), (2, 1, 10, 1), (10, 10)),
)
GROUP = 4
FACES = ((1, 0), (-1, 0), (0, 1), (0, -1))


def coefficient(values, base):
    row = lax.broadcasted_iota(I32, (8, 128), 0)
    kinetic = jnp.where(row >= 5, values * values, 0.0)
    for shift in (4, 2, 1):
        kinetic = kinetic + pltpu.roll(kinetic, shift, 0)
    return base * (1.0 + 0.5 * jnp.tanh(0.5 * kinetic))


def pieces(x):
    high = x.astype(BF16)
    rest = x - high.astype(F32)
    middle = rest.astype(BF16)
    low = (rest - middle.astype(F32)).astype(BF16)
    return high, middle, low


def one_hot(rows, index):
    row = lax.broadcasted_iota(I32, (rows, index.shape[1]), 0)
    return jnp.where(row == index, 1.0, 0.0).astype(BF16)


def dot_nt(a, b):
    return lax.dot_general(a, b, (((1,), (1,)), ((), ())), preferred_element_type=F32)


def z_up(x):
    lane = lax.broadcasted_iota(I32, (8, 128), 1)
    return jnp.where(lane == 127, 0.0, pltpu.roll(x, 127, 1))


class Patch:
    def __init__(self, field, coef, x, column):
        self.field, self.coef, self.x, self.column, self.kept = field, coef, x, column, {}

    def keep(self, key, make):
        if key not in self.kept:
            self.kept[key] = make()
        return self.kept[key]

    def value(self, dx, p):
        return self.keep(("v", dx, p), lambda: self.field[self.x + dx, self.column(p)])

    def own(self, dx, p):
        return self.keep(("c", dx, p), lambda: self.coef[self.x + dx, self.column(p)])

    def flux(self, dx, p, to_x, to_p):
        return self.keep(
            ("f", dx, p, to_x, to_p),
            lambda: (self.own(dx, p) + self.own(to_x, to_p)) * (self.value(to_x, to_p) - self.value(dx, p)),
        )

    def twice_change(self, dx, p):
        lane = lax.broadcasted_iota(I32, (8, 128), 1)
        value, own = self.value(dx, p), self.own(dx, p)
        up = (own + z_up(own)) * (z_up(value) - value)
        down = jnp.where(lane == 0, own * value, pltpu.roll(up, 1, 1))
        flux_x = self.flux(dx, p, dx + 1, p) - self.flux(dx - 1, p, dx, p)
        flux_y = self.flux(dx, p, dx, p + 1) - self.flux(dx, p - 1, dx, p)
        return flux_x + flux_y + (up - down)


def spray_kernel(
    n_a, n_r, species, velocity, diffusivity, parcels, cnt, cells, slots, faces,
    result, staying, arrivals,
    ext, base, start, first, later, source,
    vel, par, cel, slo, fac, vel3, leaving, outgoing,
    load_sem, send_sem, recv_sem, base_send, base_recv, row_send, row_recv,
):
    a, r = lax.axis_index("axial"), lax.axis_index("radial")
    high_late = lax.rem(r, GROUP) >= GROUP // 2
    opener = jnp.logical_and(a == 0, r == 0)

    def there(step_a, step_r):
        ok = None
        for step, at, size in ((step_a, a, n_a), (step_r, r, n_r)):
            if step:
                here = at < size - 1 if step > 0 else at > 0
                ok = here if ok is None else jnp.logical_and(ok, here)
        return ok

    barrier = pltpu.get_barrier_semaphore()
    total = jnp.int32(0)
    for da, dr in FACES:
        ok = there(da, dr)
        total = total + ok.astype(I32)

        @pl.when(ok)
        def _(da=da, dr=dr):
            pl.semaphore_signal(barrier, inc=1, device_id=(a + da, r + dr), device_id_type=MESH)

    loads = [pltpu.make_async_copy(species.at[f], ext.at[2:10, 2:10, f], load_sem.at[f]) for f in range(5)]
    loads += [pltpu.make_async_copy(velocity.at[k], ext.at[2:10, 2:10, 5 + k], load_sem.at[5 + k]) for k in range(3)]
    loads.append(pltpu.make_async_copy(diffusivity, base.at[2:10, 2:10, 0], load_sem.at[8]))
    own_loads = len(loads)
    for k, (src, dst) in enumerate(
        ((velocity, vel), (parcels, par), (cells, cel), (slots, slo), (faces, fac))
    ):
        loads.append(pltpu.make_async_copy(src, dst, load_sem.at[9 + k]))
    for load in loads:
        load.start()

    zero2 = jnp.zeros((2, 8, 8, 128), F32)
    zero3 = jnp.zeros((8, 2, 8, 128), F32)
    corner = jnp.zeros((8, 128), F32)

    def clear_corner(x, y):
        ext[x, y] = corner
        base[x, y] = corner[:1]

    @pl.when(a == 0)
    def _():
        ext[0:2, 2:10] = zero2
        base[0:2, 2:10] = zero2[:, :, :1]
        arrivals[0] = jnp.zeros((16, 64), F32)
        clear_corner(1, 1)
        clear_corner(1, 10)

    @pl.when(a == n_a - 1)
    def _():
        ext[10:12, 2:10] = zero2
        base[10:12, 2:10] = zero2[:, :, :1]
        arrivals[1] = jnp.zeros((16, 64), F32)
        clear_corner(10, 1)
        clear_corner(10, 10)

    @pl.when(r == 0)
    def _():
        ext[2:10, 0:2] = zero3
        base[2:10, 0:2] = zero3[:, :, :1]
        arrivals[2] = jnp.zeros((16, 64), F32)
        clear_corner(1, 1)
        clear_corner(10, 1)

    @pl.when(r == n_r - 1)
    def _():
        ext[2:10, 10:12] = zero3
        base[2:10, 10:12] = zero3[:, :, :1]
        arrivals[3] = jnp.zeros((16, 64), F32)
        clear_corner(1, 10)
        clear_corner(10, 10)

    source[...] = jnp.zeros((512, 128), F32)

    def gas_at(cell):
        width = cell.shape[1]
        depth_hot = one_hot(128, cell & 127)
        rows = jnp.dot(vel3[...], jnp.concatenate([depth_hot] * 3, axis=0), preferred_element_type=F32)
        here = lax.broadcasted_iota(I32, (64, width), 0) == (cell >> 7)
        gas = [
            jnp.sum(jnp.where(here, rows[64 * k : 64 * k + 64], 0.0), axis=0, keepdims=True) for k in range(3)
        ]
        return jnp.concatenate(gas, axis=0), here, depth_hot

    def push(old, gas):
        drag = old[4:5] * (gas - old[0:3])
        new_velocity = old[0:3] + time_step * drag
        new_mass = old[3:4] * (1.0 - time_step * old[5:6])
        new_position = old[6:9] + time_step * new_velocity
        return drag, jnp.concatenate([new_velocity, new_mass, old[4:6], new_position, old[9:16]], axis=0)

    def find_leavers():
        vel3[...] = jnp.concatenate(pieces(vel[...].reshape(192, 128)), axis=1)
        lane_cells = [cel[:, 128 * h : 128 * h + 128].astype(F32) for h in range(16)]
        stacked = jnp.concatenate([par[:, 128 * h : 128 * h + 128] for h in range(16)] + lane_cells, axis=0)
        stacked3 = jnp.concatenate(pieces(stacked), axis=1)
        leave_sum = jnp.zeros((16, 128), F32)
        moved, moved_cells = [], []
        for f in range(4):
            member = lax.broadcasted_iota(I32, (1, 64), 1)
            slot = jnp.where(member < fac[0:1, f : f + 1], slo[f : f + 1, :], -1)
            high, low_hot = slot >> 7, one_hot(128, slot & 127)
            leave_sum = leave_sum + dot_nt(one_hot(16, high), low_hot)
            picked = jnp.dot(stacked3, jnp.concatenate([low_hot] * 3, axis=0), preferred_element_type=F32)
            out = jnp.zeros((16, 64), F32)
            for h in range(16):
                out = out + jnp.where(high == h, picked[16 * h : 16 * h + 16], 0.0)
            chosen = lax.broadcasted_iota(I32, (16, 64), 0) == high
            moved.append(out)
            moved_cells.append(jnp.sum(jnp.where(chosen, picked[256:272], 0.0), axis=0, keepdims=True))
        leaving[...] = leave_sum

        for f in range(4):
            gas, _, _ = gas_at(moved_cells[f].astype(I32))
            member = lax.broadcasted_iota(I32, (1, 64), 1)
            outgoing[f] = jnp.where(member < fac[0:1, f : f + 1], push(moved[f], gas)[1], 0.0)

    def parcel_step(c, _):
        span = pl.ds(pl.multiple_of(c * CHUNK, CHUNK), CHUNK)
        gas, here, depth_hot = gas_at(cel[:, span])
        old = par[:, span]
        mass, evaporation = old[3:4], old[5:6]
        drag, new = push(old, gas)
        live = lax.broadcasted_iota(I32, (1, CHUNK), 1) + c * CHUNK < cnt[0, 0]
        leave = jnp.concatenate(
            [leaving[pl.ds(c * (CHUNK // 128) + j, 1), :] for j in range(CHUNK // 128)], axis=1
        )
        staying[:, span] = jnp.where(jnp.logical_and(live, leave == 0.0), new, 0.0)
        deposit = [mass * evaporation] + [-mass * drag[k : k + 1] for k in range(3)]
        split = [pieces(jnp.where(live, d, 0.0)) for d in deposit]
        added = jnp.zeros((256, 128), F32)
        for p in range(3):
            spread = jnp.concatenate(
                [jnp.where(here, split[k][p].astype(F32), 0.0).astype(BF16) for k in range(4)], axis=0
            )
            added = added + dot_nt(spread, depth_hot)
        source[0:64] += added[0:64]
        source[320:512] += added[64:256]
        return 0

    for load in loads:
        load.wait()

    chunks = 2048 // CHUNK
    ahead = jnp.where(opener, 0, chunks)
    pl.when(jnp.logical_not(opener))(find_leavers)
    lax.fori_loop(0, ahead, parcel_step, 0)

    pl.semaphore_wait(barrier, total)

    def trip(k):
        (da, dr), (sx, nx, sy, ny), (tx, ty) = TRIPS[k]
        device = (a + da, r + dr)
        return (
            pltpu.make_async_remote_copy(
                src_ref=ext.at[sx : sx + nx, sy : sy + ny],
                dst_ref=ext.at[tx : tx + nx, ty : ty + ny],
                send_sem=send_sem.at[k], recv_sem=recv_sem.at[k],
                device_id=device, device_id_type=MESH,
            ),
            pltpu.make_async_remote_copy(
                src_ref=base.at[sx : sx + nx, sy : sy + ny],
                dst_ref=base.at[tx : tx + nx, ty : ty + ny],
                send_sem=base_send.at[k], recv_sem=base_recv.at[k],
                device_id=device, device_id_type=MESH,
            ),
        )

    def sends(k):
        da, dr = TRIPS[k][0]
        out, back = there(da, dr), there(-da, -dr)
        if k >= 8:
            side = there(0, -1) if k < 10 else there(0, 1)
            out, back = jnp.logical_and(out, side), jnp.logical_and(back, side)
        return out, back

    def send(trips, ok=None):
        for k in trips:
            out, _ = sends(k)

            @pl.when(out if ok is None else jnp.logical_and(out, ok))
            def _(k=k):
                for copy in trip(k):
                    copy.start()

    def receive(trips, ok=None):
        for k in trips:
            _, back = sends(k)

            @pl.when(back if ok is None else jnp.logical_and(back, ok))
            def _(k=k):
                for copy in trip(k):
                    copy.wait_recv()

    to_high, to_low = lax.rem(r, GROUP) == GROUP - 1, lax.rem(r, GROUP) == 0
    send((0, 1, 2), to_high)
    send((3, 4, 5), to_low)
    send((6, 7))
    send((0, 1, 2), jnp.logical_not(to_high))
    send((3, 4, 5), jnp.logical_not(to_low))

    def row_copy(f):
        da, dr = FACES[f]
        return pltpu.make_async_remote_copy(
            src_ref=outgoing.at[f], dst_ref=arrivals.at[f],
            send_sem=row_send.at[f], recv_sem=row_recv.at[f],
            device_id=(a + da, r + dr), device_id_type=MESH,
        )

    def send_rows(ok):
        for f in (2, 3, 0, 1):

            @pl.when(jnp.logical_and(there(*FACES[f]), ok))
            def _(f=f):
                row_copy(f).start()

    send_rows(jnp.logical_not(opener))

    pl.when(opener)(find_leavers)

    def own_start(x, _):
        for y in range(2, 10):
            start[x, y] = coefficient(ext[x, y], base[x, y])
        return 0

    lax.fori_loop(2, 10, own_start, 0)
    send_rows(opener)
    low_late = jnp.logical_not(high_late)
    receive((0, 1), high_late)
    send((8, 9), high_late)
    receive((3, 4), low_late)
    send((10, 11), low_late)
    receive((3, 4), high_late)
    send((10, 11), high_late)
    receive((0, 1), low_late)
    send((8, 9), low_late)

    lax.fori_loop(ahead, chunks, parcel_step, 0)

    def find_start(x, y):
        start[x, y] = coefficient(ext[x, y], base[x, y])

    def find_first(patch, dx, p, outside):
        x, y = patch.x + dx, patch.column(p)
        new = patch.value(dx, p) + (0.5 * time_step) * patch.twice_change(dx, p)
        if outside is not None:
            new = jnp.where(outside, 0.0, new)
        first[x, y] = new
        later[x, y] = coefficient(new, base[x, y])

    def find_second(patch, dx, p):
        x, y = patch.x + dx, patch.column(p)
        cell = (x - 2) * 8 + (y - 2)
        result[pl.ds(cell, 8, stride=64), :] = (
            0.5 * (ext[x, y] + patch.value(dx, p))
            + (0.25 * time_step) * patch.twice_change(dx, p)
            + time_step * source[pl.ds(cell, 8, stride=64), :]
        )

    def repeat(low, high, step):
        def run(i, _):
            step(i)
            return 0

        lax.fori_loop(low, high, run, 0)

    def inner_first(x):
        patch = Patch(ext, start, x, lambda p: p)
        for p in range(3, 9):
            find_first(patch, 0, p, None)

    def inner_second(x):
        patch = Patch(first, later, x, lambda p: p)
        for p in range(4, 8):
            find_second(patch, 0, p)

    repeat(3, 9, inner_first)
    repeat(4, 8, inner_second)

    places = [jnp.where(high_late, p, 11 - p) for p in range(12)]

    def column(p):
        return places[p]

    early_edge = jnp.where(high_late, r == 0, r == n_r - 1)
    late_edge = jnp.where(high_late, r == n_r - 1, r == 0)

    receive((6, 7))
    receive((2, 8, 9), high_late)
    receive((5, 10, 11), low_late)

    def early_side_start(i):
        for dx in range(4):
            for p in (0, 1):
                find_start(2 + 4 * i + dx, column(p))

    def early_end_start(i):
        for p in range(2, 10):
            find_start(11 * i, column(p))
        for p in range(1, 10):
            find_start(1 + 9 * i, column(p))

    repeat(0, 2, early_side_start)
    repeat(0, 2, early_end_start)

    def early_end_first(i):
        outer = Patch(ext, start, 1 + 9 * i, column)
        for p in range(2, 9):
            find_first(outer, 0, p, jnp.where(i == 0, a == 0, a == n_a - 1))
        inner = Patch(ext, start, 2 + 7 * i, column)
        for p in range(1, 9):
            find_first(inner, 0, p, early_edge if p == 1 else None)

    def early_side_first(i):
        patch = Patch(ext, start, 3 + 3 * i, column)
        for dx in range(3):
            find_first(patch, dx, 1, early_edge)
            find_first(patch, dx, 2, None)

    repeat(0, 2, early_end_first)
    repeat(0, 2, early_side_first)

    def early_end_second(i):
        patch = Patch(first, later, 2 + 6 * i, column)
        for dx in (0, 1):
            for p in range(2, 8):
                find_second(patch, dx, p)

    def early_side_second(i):
        patch = Patch(first, later, 4 + 2 * i, column)
        for dx in (0, 1):
            for p in (2, 3):
                find_second(patch, dx, p)

    repeat(0, 2, early_end_second)
    repeat(0, 2, early_side_second)

    for f, (da, dr) in enumerate(FACES):

        @pl.when(there(-da, -dr))
        def _(f=f):
            row_copy(f).wait_recv()

    for k in range(12):

        @pl.when(sends(k)[0])
        def _(k=k):
            for copy in trip(k):
                copy.wait_send()

    for f, (da, dr) in enumerate(FACES):

        @pl.when(there(da, dr))
        def _(f=f):
            row_copy(f).wait_send()

    receive((5, 10, 11), high_late)
    receive((2, 8, 9), low_late)

    for x in range(2, 10):
        for p in (10, 11):
            find_start(x, column(p))
    for x in (1, 10):
        find_start(x, column(10))
    patch = Patch(ext, start, 0, column)
    find_first(patch, 1, 9, a == 0)
    for x in range(2, 10):
        find_first(patch, x, 9, None)
        find_first(patch, x, 10, late_edge)
    find_first(patch, 10, 9, a == n_a - 1)
    patch = Patch(first, later, 0, column)
    for x in range(2, 10):
        for p in (8, 9):
            find_second(patch, x, p)


def store_kernel(result, staying, arrivals, species_out, velocity_out, staying_out, arrivals_out, sems):
    copies = [
        pltpu.make_async_copy(src, dst, sems.at[k])
        for k, (src, dst) in enumerate(
            (
                (result.at[0:320], species_out), (result.at[320:512], velocity_out),
                (staying, staying_out), (arrivals, arrivals_out),
            )
        )
    ]
    for copy in copies:
        copy.start()
    for copy in copies:
        copy.wait()


def body(n_a, n_r, species, velocity, diffusivity, parcels, counts, cells, leave_slots, leave_counts):
    anywhere = pl.BlockSpec(memory_space=pl.ANY)
    vmem = pl.BlockSpec(memory_space=pltpu.VMEM)
    shape = lambda *dims: jax.ShapeDtypeStruct(dims, F32)
    local = lambda *dims: pltpu.VMEM(dims, F32)
    dma = pltpu.SemaphoreType.DMA
    between = pl.pallas_call(
        functools.partial(spray_kernel, n_a, n_r),
        name="spray",
        out_shape=[local(512, 128), local(16, 2048), local(4, 16, 64)],
        in_specs=[anywhere] * 4 + [pl.BlockSpec(memory_space=pltpu.SMEM)] + [anywhere] * 3,
        out_specs=[vmem] * 3,
        scratch_shapes=[
            local(12, 12, 8, 128), local(12, 12, 1, 128), local(12, 12, 8, 128), local(12, 12, 8, 128),
            local(12, 12, 8, 128), local(512, 128),
            local(3, 8, 8, 128), local(16, 2048),
            pltpu.VMEM((1, 2048), I32), pltpu.VMEM((4, 64), I32), pltpu.VMEM((1, 4), I32),
            pltpu.VMEM((192, 384), BF16), local(16, 128), local(4, 16, 64),
            dma((14,)), dma((12,)), dma((12,)), dma((12,)), dma((12,)), dma((4,)), dma((4,)),
        ],
        compiler_params=pltpu.CompilerParams(collective_id=0, has_side_effects=True),
    )(
        species, velocity, diffusivity, parcels[0, 0], counts, cells[0], leave_slots[0, 0], leave_counts[0],
    )
    species_out, velocity_out, staying, arrivals = pl.pallas_call(
        store_kernel,
        name="store",
        out_shape=[shape(320, 128), shape(192, 128), shape(16, 2048), shape(4, 16, 64)],
        in_specs=[vmem] * 3,
        out_specs=[anywhere] * 4,
        scratch_shapes=[dma((4,))],
    )(*[pltpu.with_memory_space_constraint(x, pltpu.VMEM) for x in between])
    return (
        species_out.reshape(5, 8, 8, 128), velocity_out.reshape(3, 8, 8, 128),
        staying[None, None], arrivals[None, None],
    )


def solution(mesh):
    return jax.shard_map(
        functools.partial(body, mesh.shape["axial"], mesh.shape["radial"]),
        mesh=mesh,
        in_specs=(
            P(None, "axial", "radial", None),
            P(None, "axial", "radial", None),
            P("axial", "radial", None),
            P("axial", "radial", None, None),
            P("axial", "radial"),
            P("axial", "radial", None),
            P("axial", "radial", None, None),
            P("axial", "radial", None),
        ),
        out_specs=(
            P(None, "axial", "radial", None),
            P(None, "axial", "radial", None),
            P("axial", "radial", None, None),
            P("axial", "radial", None, None, None),
        ),
        check_vma=False,
    )
```

```python
import functools

import jax
import jax.numpy as jnp
from jax import lax
from jax.experimental import pallas as pl
from jax.experimental.pallas import tpu as pltpu
from jax.sharding import PartitionSpec as P

MESH = pl.DeviceIdType.MESH
F32, BF16, I32 = jnp.float32, jnp.bfloat16, jnp.int32
time_step = 0.1
CHUNK = 512
TRIPS = (
    ((0, 1), (2, 1, 8, 2), (2, 0)), ((0, 1), (9, 1, 8, 2), (9, 0)), ((0, 1), (3, 6, 8, 2), (3, 0)),
    ((0, -1), (2, 1, 2, 2), (2, 10)), ((0, -1), (9, 1, 2, 2), (9, 10)), ((0, -1), (3, 6, 2, 2), (3, 10)),
    ((1, 0), (8, 2, 2, 8), (0, 2)), ((-1, 0), (2, 2, 2, 8), (10, 2)),
    ((1, 0), (9, 1, 1, 1), (1, 1)), ((-1, 0), (2, 1, 1, 1), (10, 1)),
    ((1, 0), (9, 1, 10, 1), (1, 10)), ((-1, 0), (2, 1, 10, 1), (10, 10)),
)
GROUP = 4
FACES = ((1, 0), (-1, 0), (0, 1), (0, -1))


def coefficient(values, base):
    row = lax.broadcasted_iota(I32, (8, 128), 0)
    kinetic = jnp.where(row >= 5, values * values, 0.0)
    for shift in (4, 2, 1):
        kinetic = kinetic + pltpu.roll(kinetic, shift, 0)
    return base * (1.0 + 0.5 * jnp.tanh(0.5 * kinetic))


def pieces(x):
    high = x.astype(BF16)
    rest = x - high.astype(F32)
    middle = rest.astype(BF16)
    low = (rest - middle.astype(F32)).astype(BF16)
    return high, middle, low


def one_hot(rows, index):
    row = lax.broadcasted_iota(I32, (rows, index.shape[1]), 0)
    return jnp.where(row == index, 1.0, 0.0).astype(BF16)


def dot_nt(a, b):
    return lax.dot_general(a, b, (((1,), (1,)), ((), ())), preferred_element_type=F32)


def z_up(x):
    lane = lax.broadcasted_iota(I32, (8, 128), 1)
    return jnp.where(lane == 127, 0.0, pltpu.roll(x, 127, 1))


class Patch:
    def __init__(self, field, coef, x, column):
        self.field, self.coef, self.x, self.column, self.kept = field, coef, x, column, {}

    def keep(self, key, make):
        if key not in self.kept:
            self.kept[key] = make()
        return self.kept[key]

    def value(self, dx, p):
        return self.keep(("v", dx, p), lambda: self.field[self.x + dx, self.column(p)])

    def own(self, dx, p):
        return self.keep(("c", dx, p), lambda: self.coef[self.x + dx, self.column(p)])

    def flux(self, dx, p, to_x, to_p):
        return self.keep(
            ("f", dx, p, to_x, to_p),
            lambda: (self.own(dx, p) + self.own(to_x, to_p)) * (self.value(to_x, to_p) - self.value(dx, p)),
        )

    def twice_change(self, dx, p):
        lane = lax.broadcasted_iota(I32, (8, 128), 1)
        value, own = self.value(dx, p), self.own(dx, p)
        up = (own + z_up(own)) * (z_up(value) - value)
        down = jnp.where(lane == 0, own * value, pltpu.roll(up, 1, 1))
        flux_x = self.flux(dx, p, dx + 1, p) - self.flux(dx - 1, p, dx, p)
        flux_y = self.flux(dx, p, dx, p + 1) - self.flux(dx, p - 1, dx, p)
        return flux_x + flux_y + (up - down)


def spray_kernel(
    n_a, n_r, species, velocity, diffusivity, parcels, cnt, cells, slots, faces,
    result, staying, arrivals,
    ext, base, start, first, later, source,
    vel, par, cel, slo, fac, vel3, leaving, outgoing,
    load_sem, send_sem, recv_sem, base_send, base_recv, row_send, row_recv,
):
    a, r = lax.axis_index("axial"), lax.axis_index("radial")
    high_late = lax.rem(r, GROUP) >= GROUP // 2
    in_group = lax.rem(r, GROUP)
    inside = jnp.logical_and(in_group != GROUP - 1, jnp.logical_and(lax.rem(a, 2) == 0, a > 0))
    opener = jnp.logical_and(a == 0, r == 0)
    eager = jnp.logical_or(jnp.logical_or(jnp.logical_and(in_group == 0, r > 0), inside), opener)

    def there(step_a, step_r):
        ok = None
        for step, at, size in ((step_a, a, n_a), (step_r, r, n_r)):
            if step:
                here = at < size - 1 if step > 0 else at > 0
                ok = here if ok is None else jnp.logical_and(ok, here)
        return ok

    barrier = pltpu.get_barrier_semaphore()
    total = jnp.int32(0)
    for da, dr in FACES:
        ok = there(da, dr)
        total = total + ok.astype(I32)

        @pl.when(ok)
        def _(da=da, dr=dr):
            pl.semaphore_signal(barrier, inc=1, device_id=(a + da, r + dr), device_id_type=MESH)

    loads = [pltpu.make_async_copy(species.at[f], ext.at[2:10, 2:10, f], load_sem.at[f]) for f in range(5)]
    loads += [pltpu.make_async_copy(velocity.at[k], ext.at[2:10, 2:10, 5 + k], load_sem.at[5 + k]) for k in range(3)]
    loads.append(pltpu.make_async_copy(diffusivity, base.at[2:10, 2:10, 0], load_sem.at[8]))
    own_loads = len(loads)
    for k, (src, dst) in enumerate(
        ((velocity, vel), (parcels, par), (cells, cel), (slots, slo), (faces, fac))
    ):
        loads.append(pltpu.make_async_copy(src, dst, load_sem.at[9 + k]))
    for load in loads:
        load.start()

    zero2 = jnp.zeros((2, 8, 8, 128), F32)
    zero3 = jnp.zeros((8, 2, 8, 128), F32)
    corner = jnp.zeros((8, 128), F32)

    def clear_corner(x, y):
        ext[x, y] = corner
        base[x, y] = corner[:1]

    @pl.when(a == 0)
    def _():
        ext[0:2, 2:10] = zero2
        base[0:2, 2:10] = zero2[:, :, :1]
        arrivals[0] = jnp.zeros((16, 64), F32)
        clear_corner(1, 1)
        clear_corner(1, 10)

    @pl.when(a == n_a - 1)
    def _():
        ext[10:12, 2:10] = zero2
        base[10:12, 2:10] = zero2[:, :, :1]
        arrivals[1] = jnp.zeros((16, 64), F32)
        clear_corner(10, 1)
        clear_corner(10, 10)

    @pl.when(r == 0)
    def _():
        ext[2:10, 0:2] = zero3
        base[2:10, 0:2] = zero3[:, :, :1]
        arrivals[2] = jnp.zeros((16, 64), F32)
        clear_corner(1, 1)
        clear_corner(10, 1)

    @pl.when(r == n_r - 1)
    def _():
        ext[2:10, 10:12] = zero3
        base[2:10, 10:12] = zero3[:, :, :1]
        arrivals[3] = jnp.zeros((16, 64), F32)
        clear_corner(1, 10)
        clear_corner(10, 10)

    source[...] = jnp.zeros((512, 128), F32)

    def gas_at(cell):
        width = cell.shape[1]
        depth_hot = one_hot(128, cell & 127)
        rows = jnp.dot(vel3[...], jnp.concatenate([depth_hot] * 3, axis=0), preferred_element_type=F32)
        here = lax.broadcasted_iota(I32, (64, width), 0) == (cell >> 7)
        gas = [
            jnp.sum(jnp.where(here, rows[64 * k : 64 * k + 64], 0.0), axis=0, keepdims=True) for k in range(3)
        ]
        return jnp.concatenate(gas, axis=0), here, depth_hot

    def push(old, gas):
        drag = old[4:5] * (gas - old[0:3])
        new_velocity = old[0:3] + time_step * drag
        new_mass = old[3:4] * (1.0 - time_step * old[5:6])
        new_position = old[6:9] + time_step * new_velocity
        return drag, jnp.concatenate([new_velocity, new_mass, old[4:6], new_position, old[9:16]], axis=0)

    def find_leavers():
        vel3[...] = jnp.concatenate(pieces(vel[...].reshape(192, 128)), axis=1)
        lane_cells = [cel[:, 128 * h : 128 * h + 128].astype(F32) for h in range(16)]
        stacked = jnp.concatenate([par[:, 128 * h : 128 * h + 128] for h in range(16)] + lane_cells, axis=0)
        stacked3 = jnp.concatenate(pieces(stacked), axis=1)
        leave_sum = jnp.zeros((16, 128), F32)
        moved, moved_cells = [], []
        for f in range(4):
            member = lax.broadcasted_iota(I32, (1, 64), 1)
            slot = jnp.where(member < fac[0:1, f : f + 1], slo[f : f + 1, :], -1)
            high, low_hot = slot >> 7, one_hot(128, slot & 127)
            leave_sum = leave_sum + dot_nt(one_hot(16, high), low_hot)
            picked = jnp.dot(stacked3, jnp.concatenate([low_hot] * 3, axis=0), preferred_element_type=F32)
            out = jnp.zeros((16, 64), F32)
            for h in range(16):
                out = out + jnp.where(high == h, picked[16 * h : 16 * h + 16], 0.0)
            chosen = lax.broadcasted_iota(I32, (16, 64), 0) == high
            moved.append(out)
            moved_cells.append(jnp.sum(jnp.where(chosen, picked[256:272], 0.0), axis=0, keepdims=True))
        leaving[...] = leave_sum

        for f in range(4):
            gas, _, _ = gas_at(moved_cells[f].astype(I32))
            member = lax.broadcasted_iota(I32, (1, 64), 1)
            outgoing[f] = jnp.where(member < fac[0:1, f : f + 1], push(moved[f], gas)[1], 0.0)

    def parcel_step(c, _):
        span = pl.ds(pl.multiple_of(c * CHUNK, CHUNK), CHUNK)
        gas, here, depth_hot = gas_at(cel[:, span])
        old = par[:, span]
        mass, evaporation = old[3:4], old[5:6]
        drag, new = push(old, gas)
        live = lax.broadcasted_iota(I32, (1, CHUNK), 1) + c * CHUNK < cnt[0, 0]
        leave = jnp.concatenate(
            [leaving[pl.ds(c * (CHUNK // 128) + j, 1), :] for j in range(CHUNK // 128)], axis=1
        )
        staying[:, span] = jnp.where(jnp.logical_and(live, leave == 0.0), new, 0.0)
        deposit = [mass * evaporation] + [-mass * drag[k : k + 1] for k in range(3)]
        split = [pieces(jnp.where(live, d, 0.0)) for d in deposit]
        added = jnp.zeros((256, 128), F32)
        for p in range(3):
            spread = jnp.concatenate(
                [jnp.where(here, split[k][p].astype(F32), 0.0).astype(BF16) for k in range(4)], axis=0
            )
            added = added + dot_nt(spread, depth_hot)
        source[0:64] += added[0:64]
        source[320:512] += added[64:256]
        return 0

    for load in loads:
        load.wait()

    chunks = 2048 // CHUNK
    ahead = jnp.where(eager, 0, chunks)
    pl.when(jnp.logical_not(eager))(find_leavers)
    lax.fori_loop(0, ahead, parcel_step, 0)

    pl.semaphore_wait(barrier, total)

    def trip(k):
        (da, dr), (sx, nx, sy, ny), (tx, ty) = TRIPS[k]
        device = (a + da, r + dr)
        return (
            pltpu.make_async_remote_copy(
                src_ref=ext.at[sx : sx + nx, sy : sy + ny],
                dst_ref=ext.at[tx : tx + nx, ty : ty + ny],
                send_sem=send_sem.at[k], recv_sem=recv_sem.at[k],
                device_id=device, device_id_type=MESH,
            ),
            pltpu.make_async_remote_copy(
                src_ref=base.at[sx : sx + nx, sy : sy + ny],
                dst_ref=base.at[tx : tx + nx, ty : ty + ny],
                send_sem=base_send.at[k], recv_sem=base_recv.at[k],
                device_id=device, device_id_type=MESH,
            ),
        )

    def sends(k):
        da, dr = TRIPS[k][0]
        out, back = there(da, dr), there(-da, -dr)
        if k >= 8:
            side = there(0, -1) if k < 10 else there(0, 1)
            out, back = jnp.logical_and(out, side), jnp.logical_and(back, side)
        return out, back

    def send(trips, ok=None):
        for k in trips:
            out, _ = sends(k)

            @pl.when(out if ok is None else jnp.logical_and(out, ok))
            def _(k=k):
                for copy in trip(k):
                    copy.start()

    def receive(trips, ok=None):
        for k in trips:
            _, back = sends(k)

            @pl.when(back if ok is None else jnp.logical_and(back, ok))
            def _(k=k):
                for copy in trip(k):
                    copy.wait_recv()

    to_high, to_low = lax.rem(r, GROUP) == GROUP - 1, lax.rem(r, GROUP) == 0
    send((0, 1, 2), to_high)
    send((3, 4, 5), to_low)
    send((6, 7))
    send((0, 1, 2), jnp.logical_not(to_high))
    send((3, 4, 5), jnp.logical_not(to_low))

    def row_copy(f):
        da, dr = FACES[f]
        return pltpu.make_async_remote_copy(
            src_ref=outgoing.at[f], dst_ref=arrivals.at[f],
            send_sem=row_send.at[f], recv_sem=row_recv.at[f],
            device_id=(a + da, r + dr), device_id_type=MESH,
        )

    def send_rows(ok):
        for f in (2, 3, 0, 1):

            @pl.when(jnp.logical_and(there(*FACES[f]), ok))
            def _(f=f):
                row_copy(f).start()

    send_rows(jnp.logical_not(eager))

    pl.when(eager)(find_leavers)

    def own_start(x, _):
        for y in range(2, 10):
            start[x, y] = coefficient(ext[x, y], base[x, y])
        return 0

    lax.fori_loop(2, 10, own_start, 0)
    send_rows(eager)
    low_late = jnp.logical_not(high_late)

    def hand_on(ok, early):
        for is_high in (False, True):
            chosen = jnp.logical_and(ok, low_late if is_high == early else high_late)
            receive((3, 4) if is_high else (0, 1), chosen)
            send((10, 11) if is_high else (8, 9), chosen)

    hand_on(eager, True)
    lax.fori_loop(ahead, chunks, parcel_step, 0)

    def find_start(x, y):
        start[x, y] = coefficient(ext[x, y], base[x, y])

    def find_first(patch, dx, p, outside):
        x, y = patch.x + dx, patch.column(p)
        new = patch.value(dx, p) + (0.5 * time_step) * patch.twice_change(dx, p)
        if outside is not None:
            new = jnp.where(outside, 0.0, new)
        first[x, y] = new
        later[x, y] = coefficient(new, base[x, y])

    def find_second(patch, dx, p):
        x, y = patch.x + dx, patch.column(p)
        cell = (x - 2) * 8 + (y - 2)
        result[pl.ds(cell, 8, stride=64), :] = (
            0.5 * (ext[x, y] + patch.value(dx, p))
            + (0.25 * time_step) * patch.twice_change(dx, p)
            + time_step * source[pl.ds(cell, 8, stride=64), :]
        )

    def repeat(low, high, step):
        def run(i, _):
            step(i)
            return 0

        lax.fori_loop(low, high, run, 0)

    def inner_first(x):
        patch = Patch(ext, start, x, lambda p: p)
        for p in range(3, 9):
            find_first(patch, 0, p, None)

    def inner_second(x):
        patch = Patch(first, later, x, lambda p: p)
        for p in range(4, 8):
            find_second(patch, 0, p)

    repeat(3, 9, inner_first)
    repeat(4, 8, inner_second)
    hand_on(jnp.logical_not(eager), True)
    hand_on(jnp.bool_(True), False)

    places = [jnp.where(high_late, p, 11 - p) for p in range(12)]

    def column(p):
        return places[p]

    early_edge = jnp.where(high_late, r == 0, r == n_r - 1)
    late_edge = jnp.where(high_late, r == n_r - 1, r == 0)

    receive((6, 7))
    receive((2, 8, 9), high_late)
    receive((5, 10, 11), low_late)

    def early_side_start(i):
        for dx in range(4):
            for p in (0, 1):
                find_start(2 + 4 * i + dx, column(p))

    def early_end_start(i):
        for p in range(2, 10):
            find_start(11 * i, column(p))
        for p in range(1, 10):
            find_start(1 + 9 * i, column(p))

    repeat(0, 2, early_side_start)
    repeat(0, 2, early_end_start)

    def early_end_first(i):
        outer = Patch(ext, start, 1 + 9 * i, column)
        for p in range(2, 9):
            find_first(outer, 0, p, jnp.where(i == 0, a == 0, a == n_a - 1))
        inner = Patch(ext, start, 2 + 7 * i, column)
        for p in range(1, 9):
            find_first(inner, 0, p, early_edge if p == 1 else None)

    def early_side_first(i):
        patch = Patch(ext, start, 3 + 3 * i, column)
        for dx in range(3):
            find_first(patch, dx, 1, early_edge)
            find_first(patch, dx, 2, None)

    repeat(0, 2, early_end_first)
    repeat(0, 2, early_side_first)

    def early_end_second(i):
        patch = Patch(first, later, 2 + 6 * i, column)
        for dx in (0, 1):
            for p in range(2, 8):
                find_second(patch, dx, p)

    def early_side_second(i):
        patch = Patch(first, later, 4 + 2 * i, column)
        for dx in (0, 1):
            for p in (2, 3):
                find_second(patch, dx, p)

    repeat(0, 2, early_end_second)
    repeat(0, 2, early_side_second)

    for f, (da, dr) in enumerate(FACES):

        @pl.when(there(-da, -dr))
        def _(f=f):
            row_copy(f).wait_recv()

    for k in range(12):

        @pl.when(sends(k)[0])
        def _(k=k):
            for copy in trip(k):
                copy.wait_send()

    for f, (da, dr) in enumerate(FACES):

        @pl.when(there(da, dr))
        def _(f=f):
            row_copy(f).wait_send()

    receive((5, 10, 11), high_late)
    receive((2, 8, 9), low_late)

    for x in range(2, 10):
        for p in (10, 11):
            find_start(x, column(p))
    for x in (1, 10):
        find_start(x, column(10))
    patch = Patch(ext, start, 0, column)
    find_first(patch, 1, 9, a == 0)
    for x in range(2, 10):
        find_first(patch, x, 9, None)
        find_first(patch, x, 10, late_edge)
    find_first(patch, 10, 9, a == n_a - 1)
    patch = Patch(first, later, 0, column)
    for x in range(2, 10):
        for p in (8, 9):
            find_second(patch, x, p)


def store_kernel(result, staying, arrivals, species_out, velocity_out, staying_out, arrivals_out, sems):
    copies = [
        pltpu.make_async_copy(src, dst, sems.at[k])
        for k, (src, dst) in enumerate(
            (
                (result.at[0:320], species_out), (result.at[320:512], velocity_out),
                (staying, staying_out), (arrivals, arrivals_out),
            )
        )
    ]
    for copy in copies:
        copy.start()
    for copy in copies:
        copy.wait()


def body(n_a, n_r, species, velocity, diffusivity, parcels, counts, cells, leave_slots, leave_counts):
    anywhere = pl.BlockSpec(memory_space=pl.ANY)
    vmem = pl.BlockSpec(memory_space=pltpu.VMEM)
    shape = lambda *dims: jax.ShapeDtypeStruct(dims, F32)
    local = lambda *dims: pltpu.VMEM(dims, F32)
    dma = pltpu.SemaphoreType.DMA
    between = pl.pallas_call(
        functools.partial(spray_kernel, n_a, n_r),
        name="spray",
        out_shape=[local(512, 128), local(16, 2048), local(4, 16, 64)],
        in_specs=[anywhere] * 4 + [pl.BlockSpec(memory_space=pltpu.SMEM)] + [anywhere] * 3,
        out_specs=[vmem] * 3,
        scratch_shapes=[
            local(12, 12, 8, 128), local(12, 12, 1, 128), local(12, 12, 8, 128), local(12, 12, 8, 128),
            local(12, 12, 8, 128), local(512, 128),
            local(3, 8, 8, 128), local(16, 2048),
            pltpu.VMEM((1, 2048), I32), pltpu.VMEM((4, 64), I32), pltpu.VMEM((1, 4), I32),
            pltpu.VMEM((192, 384), BF16), local(16, 128), local(4, 16, 64),
            dma((14,)), dma((12,)), dma((12,)), dma((12,)), dma((12,)), dma((4,)), dma((4,)),
        ],
        compiler_params=pltpu.CompilerParams(collective_id=0, has_side_effects=True),
    )(
        species, velocity, diffusivity, parcels[0, 0], counts, cells[0], leave_slots[0, 0], leave_counts[0],
    )
    species_out, velocity_out, staying, arrivals = pl.pallas_call(
        store_kernel,
        name="store",
        out_shape=[shape(320, 128), shape(192, 128), shape(16, 2048), shape(4, 16, 64)],
        in_specs=[vmem] * 3,
        out_specs=[anywhere] * 4,
        scratch_shapes=[dma((4,))],
    )(*[pltpu.with_memory_space_constraint(x, pltpu.VMEM) for x in between])
    return (
        species_out.reshape(5, 8, 8, 128), velocity_out.reshape(3, 8, 8, 128),
        staying[None, None], arrivals[None, None],
    )


def solution(mesh):
    return jax.shard_map(
        functools.partial(body, mesh.shape["axial"], mesh.shape["radial"]),
        mesh=mesh,
        in_specs=(
            P(None, "axial", "radial", None),
            P(None, "axial", "radial", None),
            P("axial", "radial", None),
            P("axial", "radial", None, None),
            P("axial", "radial"),
            P("axial", "radial", None),
            P("axial", "radial", None, None),
            P("axial", "radial", None),
        ),
        out_specs=(
            P(None, "axial", "radial", None),
            P(None, "axial", "radial", None),
            P("axial", "radial", None, None),
            P("axial", "radial", None, None, None),
        ),
        check_vma=False,
    )
```

```python
import functools

import jax
import jax.numpy as jnp
from jax import lax
from jax.experimental import pallas as pl
from jax.experimental.pallas import tpu as pltpu
from jax.sharding import PartitionSpec as P

MESH = pl.DeviceIdType.MESH
F32, BF16, I32 = jnp.float32, jnp.bfloat16, jnp.int32
time_step = 0.1
CHUNK = 512
TRIPS = (
    ((0, 1), (2, 1, 8, 2), (2, 0)), ((0, 1), (9, 1, 8, 2), (9, 0)), ((0, 1), (3, 6, 8, 2), (3, 0)),
    ((0, -1), (2, 1, 2, 2), (2, 10)), ((0, -1), (9, 1, 2, 2), (9, 10)), ((0, -1), (3, 6, 2, 2), (3, 10)),
    ((1, 0), (8, 2, 2, 8), (0, 2)), ((-1, 0), (2, 2, 2, 8), (10, 2)),
    ((1, 0), (9, 1, 1, 1), (1, 1)), ((-1, 0), (2, 1, 1, 1), (10, 1)),
    ((1, 0), (9, 1, 10, 1), (1, 10)), ((-1, 0), (2, 1, 10, 1), (10, 10)),
)
GROUP = 4
FACES = ((1, 0), (-1, 0), (0, 1), (0, -1))


def coefficient(values, base):
    row = lax.broadcasted_iota(I32, (8, 128), 0)
    kinetic = jnp.where(row >= 5, values * values, 0.0)
    for shift in (4, 2, 1):
        kinetic = kinetic + pltpu.roll(kinetic, shift, 0)
    return base * (1.0 + 0.5 * jnp.tanh(0.5 * kinetic))


def pieces(x):
    high = x.astype(BF16)
    rest = x - high.astype(F32)
    middle = rest.astype(BF16)
    low = (rest - middle.astype(F32)).astype(BF16)
    return high, middle, low


def one_hot(rows, index):
    row = lax.broadcasted_iota(I32, (rows, index.shape[1]), 0)
    return jnp.where(row == index, 1.0, 0.0).astype(BF16)


def dot_nt(a, b):
    return lax.dot_general(a, b, (((1,), (1,)), ((), ())), preferred_element_type=F32)


def z_up(x):
    lane = lax.broadcasted_iota(I32, (8, 128), 1)
    return jnp.where(lane == 127, 0.0, pltpu.roll(x, 127, 1))


class Patch:
    def __init__(self, field, coef, x, column):
        self.field, self.coef, self.x, self.column, self.kept = field, coef, x, column, {}

    def keep(self, key, make):
        if key not in self.kept:
            self.kept[key] = make()
        return self.kept[key]

    def value(self, dx, p):
        return self.keep(("v", dx, p), lambda: self.field[self.x + dx, self.column(p)])

    def own(self, dx, p):
        return self.keep(("c", dx, p), lambda: self.coef[self.x + dx, self.column(p)])

    def flux(self, dx, p, to_x, to_p):
        return self.keep(
            ("f", dx, p, to_x, to_p),
            lambda: (self.own(dx, p) + self.own(to_x, to_p)) * (self.value(to_x, to_p) - self.value(dx, p)),
        )

    def twice_change(self, dx, p):
        lane = lax.broadcasted_iota(I32, (8, 128), 1)
        value, own = self.value(dx, p), self.own(dx, p)
        up = (own + z_up(own)) * (z_up(value) - value)
        down = jnp.where(lane == 0, own * value, pltpu.roll(up, 1, 1))
        flux_x = self.flux(dx, p, dx + 1, p) - self.flux(dx - 1, p, dx, p)
        flux_y = self.flux(dx, p, dx, p + 1) - self.flux(dx, p - 1, dx, p)
        return flux_x + flux_y + (up - down)


def spray_kernel(
    n_a, n_r, species, velocity, diffusivity, parcels, cnt, cells, slots, faces,
    result, staying, arrivals,
    ext, base, start, first, later, source,
    vel, par, cel, slo, fac, vel3, leaving, outgoing,
    load_sem, send_sem, recv_sem, base_send, base_recv, row_send, row_recv,
):
    a, r = lax.axis_index("axial"), lax.axis_index("radial")
    high_late = lax.rem(r, GROUP) >= GROUP // 2
    in_group = lax.rem(r, GROUP)
    inside = jnp.logical_and(in_group != GROUP - 1, jnp.logical_and(lax.rem(a, 2) == 0, a > 0))
    opener = jnp.logical_and(a == 0, r == 0)
    eager = jnp.logical_or(jnp.logical_or(jnp.logical_and(in_group == 0, r > 0), inside), opener)

    def there(step_a, step_r):
        ok = None
        for step, at, size in ((step_a, a, n_a), (step_r, r, n_r)):
            if step:
                here = at < size - 1 if step > 0 else at > 0
                ok = here if ok is None else jnp.logical_and(ok, here)
        return ok

    barrier = pltpu.get_barrier_semaphore()
    total = jnp.int32(0)
    for da, dr in FACES:
        ok = there(da, dr)
        total = total + ok.astype(I32)

        @pl.when(ok)
        def _(da=da, dr=dr):
            pl.semaphore_signal(barrier, inc=1, device_id=(a + da, r + dr), device_id_type=MESH)

    loads = [pltpu.make_async_copy(species.at[f], ext.at[2:10, 2:10, f], load_sem.at[f]) for f in range(5)]
    loads += [pltpu.make_async_copy(velocity.at[k], ext.at[2:10, 2:10, 5 + k], load_sem.at[5 + k]) for k in range(3)]
    loads.append(pltpu.make_async_copy(diffusivity, base.at[2:10, 2:10, 0], load_sem.at[8]))
    own_loads = len(loads)
    for k, (src, dst) in enumerate(
        ((velocity, vel), (parcels, par), (cells, cel), (slots, slo), (faces, fac))
    ):
        loads.append(pltpu.make_async_copy(src, dst, load_sem.at[9 + k]))
    for load in loads:
        load.start()

    zero2 = jnp.zeros((2, 8, 8, 128), F32)
    zero3 = jnp.zeros((8, 2, 8, 128), F32)
    corner = jnp.zeros((8, 128), F32)

    def clear_corner(x, y):
        ext[x, y] = corner
        base[x, y] = corner[:1]

    @pl.when(a == 0)
    def _():
        ext[0:2, 2:10] = zero2
        base[0:2, 2:10] = zero2[:, :, :1]
        arrivals[0] = jnp.zeros((16, 64), F32)
        clear_corner(1, 1)
        clear_corner(1, 10)

    @pl.when(a == n_a - 1)
    def _():
        ext[10:12, 2:10] = zero2
        base[10:12, 2:10] = zero2[:, :, :1]
        arrivals[1] = jnp.zeros((16, 64), F32)
        clear_corner(10, 1)
        clear_corner(10, 10)

    @pl.when(r == 0)
    def _():
        ext[2:10, 0:2] = zero3
        base[2:10, 0:2] = zero3[:, :, :1]
        arrivals[2] = jnp.zeros((16, 64), F32)
        clear_corner(1, 1)
        clear_corner(10, 1)

    @pl.when(r == n_r - 1)
    def _():
        ext[2:10, 10:12] = zero3
        base[2:10, 10:12] = zero3[:, :, :1]
        arrivals[3] = jnp.zeros((16, 64), F32)
        clear_corner(1, 10)
        clear_corner(10, 10)

    source[...] = jnp.zeros((512, 128), F32)

    def gas_at(cell):
        width = cell.shape[1]
        depth_hot = one_hot(128, cell & 127)
        rows = jnp.dot(vel3[...], jnp.concatenate([depth_hot] * 3, axis=0), preferred_element_type=F32)
        here = lax.broadcasted_iota(I32, (64, width), 0) == (cell >> 7)
        gas = [
            jnp.sum(jnp.where(here, rows[64 * k : 64 * k + 64], 0.0), axis=0, keepdims=True) for k in range(3)
        ]
        return jnp.concatenate(gas, axis=0), here, depth_hot

    def push(old, gas):
        drag = old[4:5] * (gas - old[0:3])
        new_velocity = old[0:3] + time_step * drag
        new_mass = old[3:4] * (1.0 - time_step * old[5:6])
        new_position = old[6:9] + time_step * new_velocity
        return drag, jnp.concatenate([new_velocity, new_mass, old[4:6], new_position, old[9:16]], axis=0)

    def find_leavers():
        vel3[...] = jnp.concatenate(pieces(vel[...].reshape(192, 128)), axis=1)
        lane_cells = [cel[:, 128 * h : 128 * h + 128].astype(F32) for h in range(16)]
        stacked = jnp.concatenate([par[:, 128 * h : 128 * h + 128] for h in range(16)] + lane_cells, axis=0)
        stacked3 = jnp.concatenate(pieces(stacked), axis=1)
        leave_sum = jnp.zeros((16, 128), F32)
        moved, moved_cells = [], []
        for f in range(4):
            member = lax.broadcasted_iota(I32, (1, 64), 1)
            slot = jnp.where(member < fac[0:1, f : f + 1], slo[f : f + 1, :], -1)
            high, low_hot = slot >> 7, one_hot(128, slot & 127)
            leave_sum = leave_sum + dot_nt(one_hot(16, high), low_hot)
            picked = jnp.dot(stacked3, jnp.concatenate([low_hot] * 3, axis=0), preferred_element_type=F32)
            out = jnp.zeros((16, 64), F32)
            for h in range(16):
                out = out + jnp.where(high == h, picked[16 * h : 16 * h + 16], 0.0)
            chosen = lax.broadcasted_iota(I32, (16, 64), 0) == high
            moved.append(out)
            moved_cells.append(jnp.sum(jnp.where(chosen, picked[256:272], 0.0), axis=0, keepdims=True))
        leaving[...] = leave_sum

        for f in range(4):
            gas, _, _ = gas_at(moved_cells[f].astype(I32))
            member = lax.broadcasted_iota(I32, (1, 64), 1)
            outgoing[f] = jnp.where(member < fac[0:1, f : f + 1], push(moved[f], gas)[1], 0.0)

    def parcel_step(c, _):
        span = pl.ds(pl.multiple_of(c * CHUNK, CHUNK), CHUNK)
        gas, here, depth_hot = gas_at(cel[:, span])
        old = par[:, span]
        mass, evaporation = old[3:4], old[5:6]
        drag, new = push(old, gas)
        live = lax.broadcasted_iota(I32, (1, CHUNK), 1) + c * CHUNK < cnt[0, 0]
        leave = jnp.concatenate(
            [leaving[pl.ds(c * (CHUNK // 128) + j, 1), :] for j in range(CHUNK // 128)], axis=1
        )
        staying[:, span] = jnp.where(jnp.logical_and(live, leave == 0.0), new, 0.0)
        deposit = [mass * evaporation] + [-mass * drag[k : k + 1] for k in range(3)]
        split = [pieces(jnp.where(live, d, 0.0)) for d in deposit]
        added = jnp.zeros((256, 128), F32)
        for p in range(3):
            spread = jnp.concatenate(
                [jnp.where(here, split[k][p].astype(F32), 0.0).astype(BF16) for k in range(4)], axis=0
            )
            added = added + dot_nt(spread, depth_hot)
        source[0:64] += added[0:64]
        source[320:512] += added[64:256]
        return 0

    for load in loads:
        load.wait()

    chunks = 2048 // CHUNK
    ahead = jnp.where(eager, 0, chunks)
    pl.when(jnp.logical_not(eager))(find_leavers)
    lax.fori_loop(0, ahead, parcel_step, 0)

    pl.semaphore_wait(barrier, total)

    def trip(k):
        (da, dr), (sx, nx, sy, ny), (tx, ty) = TRIPS[k]
        device = (a + da, r + dr)
        return (
            pltpu.make_async_remote_copy(
                src_ref=ext.at[sx : sx + nx, sy : sy + ny],
                dst_ref=ext.at[tx : tx + nx, ty : ty + ny],
                send_sem=send_sem.at[k], recv_sem=recv_sem.at[k],
                device_id=device, device_id_type=MESH,
            ),
            pltpu.make_async_remote_copy(
                src_ref=base.at[sx : sx + nx, sy : sy + ny],
                dst_ref=base.at[tx : tx + nx, ty : ty + ny],
                send_sem=base_send.at[k], recv_sem=base_recv.at[k],
                device_id=device, device_id_type=MESH,
            ),
        )

    def sends(k):
        da, dr = TRIPS[k][0]
        out, back = there(da, dr), there(-da, -dr)
        if k >= 8:
            side = there(0, -1) if k < 10 else there(0, 1)
            out, back = jnp.logical_and(out, side), jnp.logical_and(back, side)
        return out, back

    def send(trips, ok=None):
        for k in trips:
            out, _ = sends(k)

            @pl.when(out if ok is None else jnp.logical_and(out, ok))
            def _(k=k):
                for copy in trip(k):
                    copy.start()

    def receive(trips, ok=None):
        for k in trips:
            _, back = sends(k)

            @pl.when(back if ok is None else jnp.logical_and(back, ok))
            def _(k=k):
                for copy in trip(k):
                    copy.wait_recv()

    to_high, to_low = lax.rem(r, GROUP) == GROUP - 1, lax.rem(r, GROUP) == 0
    send((0, 1), to_high)
    send((3, 4), to_low)
    even = lax.rem(a, 2) == 0
    send((5,), jnp.logical_and(to_low, even))
    send((6, 7))
    send((2,), jnp.logical_and(to_high, even))
    send((0, 1, 2), jnp.logical_not(to_high))
    send((3, 4, 5), jnp.logical_not(to_low))

    def row_copy(f):
        da, dr = FACES[f]
        return pltpu.make_async_remote_copy(
            src_ref=outgoing.at[f], dst_ref=arrivals.at[f],
            send_sem=row_send.at[f], recv_sem=row_recv.at[f],
            device_id=(a + da, r + dr), device_id_type=MESH,
        )

    def send_rows(ok):
        for f in (2, 3, 0, 1):

            @pl.when(jnp.logical_and(there(*FACES[f]), ok))
            def _(f=f):
                row_copy(f).start()

    send_rows(jnp.logical_not(eager))

    pl.when(eager)(find_leavers)

    def own_start(x, _):
        for y in range(2, 10):
            start[x, y] = coefficient(ext[x, y], base[x, y])
        return 0

    lax.fori_loop(2, 10, own_start, 0)
    send_rows(eager)
    send((2,), jnp.logical_and(to_high, jnp.logical_not(even)))
    send((5,), jnp.logical_and(to_low, jnp.logical_not(even)))
    low_late = jnp.logical_not(high_late)

    def hand_on(ok, early):
        for is_high in (False, True):
            chosen = jnp.logical_and(ok, low_late if is_high == early else high_late)
            receive((3, 4) if is_high else (0, 1), chosen)
            send((10, 11) if is_high else (8, 9), chosen)

    hand_on(eager, True)
    lax.fori_loop(ahead, chunks, parcel_step, 0)

    def find_start(x, y):
        start[x, y] = coefficient(ext[x, y], base[x, y])

    def find_first(patch, dx, p, outside):
        x, y = patch.x + dx, patch.column(p)
        new = patch.value(dx, p) + (0.5 * time_step) * patch.twice_change(dx, p)
        if outside is not None:
            new = jnp.where(outside, 0.0, new)
        first[x, y] = new
        later[x, y] = coefficient(new, base[x, y])

    def find_second(patch, dx, p):
        x, y = patch.x + dx, patch.column(p)
        cell = (x - 2) * 8 + (y - 2)
        result[pl.ds(cell, 8, stride=64), :] = (
            0.5 * (ext[x, y] + patch.value(dx, p))
            + (0.25 * time_step) * patch.twice_change(dx, p)
            + time_step * source[pl.ds(cell, 8, stride=64), :]
        )

    def repeat(low, high, step):
        def run(i, _):
            step(i)
            return 0

        lax.fori_loop(low, high, run, 0)

    def inner_first(x):
        patch = Patch(ext, start, x, lambda p: p)
        for p in range(3, 9):
            find_first(patch, 0, p, None)

    def inner_second(x):
        patch = Patch(first, later, x, lambda p: p)
        for p in range(4, 8):
            find_second(patch, 0, p)

    repeat(3, 9, inner_first)
    repeat(4, 8, inner_second)
    hand_on(jnp.logical_not(eager), True)
    hand_on(jnp.bool_(True), False)

    places = [jnp.where(high_late, p, 11 - p) for p in range(12)]

    def column(p):
        return places[p]

    early_edge = jnp.where(high_late, r == 0, r == n_r - 1)
    late_edge = jnp.where(high_late, r == n_r - 1, r == 0)

    receive((6, 7))
    receive((2, 8, 9), high_late)
    receive((5, 10, 11), low_late)

    def early_side_start(i):
        for dx in range(4):
            for p in (0, 1):
                find_start(2 + 4 * i + dx, column(p))

    def early_end_start(i):
        for p in range(2, 10):
            find_start(11 * i, column(p))
        for p in range(1, 10):
            find_start(1 + 9 * i, column(p))

    repeat(0, 2, early_side_start)
    repeat(0, 2, early_end_start)

    def early_end_first(i):
        outer = Patch(ext, start, 1 + 9 * i, column)
        for p in range(2, 9):
            find_first(outer, 0, p, jnp.where(i == 0, a == 0, a == n_a - 1))
        inner = Patch(ext, start, 2 + 7 * i, column)
        for p in range(1, 9):
            find_first(inner, 0, p, early_edge if p == 1 else None)

    def early_side_first(i):
        patch = Patch(ext, start, 3 + 3 * i, column)
        for dx in range(3):
            find_first(patch, dx, 1, early_edge)
            find_first(patch, dx, 2, None)

    repeat(0, 2, early_end_first)
    repeat(0, 2, early_side_first)

    def early_end_second(i):
        patch = Patch(first, later, 2 + 6 * i, column)
        for dx in (0, 1):
            for p in range(2, 8):
                find_second(patch, dx, p)

    def early_side_second(i):
        patch = Patch(first, later, 4 + 2 * i, column)
        for dx in (0, 1):
            for p in (2, 3):
                find_second(patch, dx, p)

    repeat(0, 2, early_end_second)
    repeat(0, 2, early_side_second)

    receive((5, 10, 11), high_late)
    receive((2, 8, 9), low_late)

    for x in range(2, 10):
        for p in (10, 11):
            find_start(x, column(p))
    for x in (1, 10):
        find_start(x, column(10))
    patch = Patch(ext, start, 0, column)
    find_first(patch, 1, 9, a == 0)
    for x in range(2, 10):
        find_first(patch, x, 9, None)
        find_first(patch, x, 10, late_edge)
    find_first(patch, 10, 9, a == n_a - 1)
    patch = Patch(first, later, 0, column)
    for x in range(2, 10):
        for p in (8, 9):
            find_second(patch, x, p)

    for f, (da, dr) in enumerate(FACES):

        @pl.when(there(-da, -dr))
        def _(f=f):
            row_copy(f).wait_recv()

    for k in range(12):

        @pl.when(sends(k)[0])
        def _(k=k):
            for copy in trip(k):
                copy.wait_send()

    for f, (da, dr) in enumerate(FACES):

        @pl.when(there(da, dr))
        def _(f=f):
            row_copy(f).wait_send()


def store_kernel(result, staying, arrivals, species_out, velocity_out, staying_out, arrivals_out, sems):
    copies = [
        pltpu.make_async_copy(src, dst, sems.at[k])
        for k, (src, dst) in enumerate(
            (
                (result.at[0:320], species_out), (result.at[320:512], velocity_out),
                (staying, staying_out), (arrivals, arrivals_out),
            )
        )
    ]
    for copy in copies:
        copy.start()
    for copy in copies:
        copy.wait()


def body(n_a, n_r, species, velocity, diffusivity, parcels, counts, cells, leave_slots, leave_counts):
    anywhere = pl.BlockSpec(memory_space=pl.ANY)
    vmem = pl.BlockSpec(memory_space=pltpu.VMEM)
    shape = lambda *dims: jax.ShapeDtypeStruct(dims, F32)
    local = lambda *dims: pltpu.VMEM(dims, F32)
    dma = pltpu.SemaphoreType.DMA
    between = pl.pallas_call(
        functools.partial(spray_kernel, n_a, n_r),
        name="spray",
        out_shape=[local(512, 128), local(16, 2048), local(4, 16, 64)],
        in_specs=[anywhere] * 4 + [pl.BlockSpec(memory_space=pltpu.SMEM)] + [anywhere] * 3,
        out_specs=[vmem] * 3,
        scratch_shapes=[
            local(12, 12, 8, 128), local(12, 12, 1, 128), local(12, 12, 8, 128), local(12, 12, 8, 128),
            local(12, 12, 8, 128), local(512, 128),
            local(3, 8, 8, 128), local(16, 2048),
            pltpu.VMEM((1, 2048), I32), pltpu.VMEM((4, 64), I32), pltpu.VMEM((1, 4), I32),
            pltpu.VMEM((192, 384), BF16), local(16, 128), local(4, 16, 64),
            dma((14,)), dma((12,)), dma((12,)), dma((12,)), dma((12,)), dma((4,)), dma((4,)),
        ],
        compiler_params=pltpu.CompilerParams(collective_id=0, has_side_effects=True),
    )(
        species, velocity, diffusivity, parcels[0, 0], counts, cells[0], leave_slots[0, 0], leave_counts[0],
    )
    species_out, velocity_out, staying, arrivals = pl.pallas_call(
        store_kernel,
        name="store",
        out_shape=[shape(320, 128), shape(192, 128), shape(16, 2048), shape(4, 16, 64)],
        in_specs=[vmem] * 3,
        out_specs=[anywhere] * 4,
        scratch_shapes=[dma((4,))],
    )(*[pltpu.with_memory_space_constraint(x, pltpu.VMEM) for x in between])
    return (
        species_out.reshape(5, 8, 8, 128), velocity_out.reshape(3, 8, 8, 128),
        staying[None, None], arrivals[None, None],
    )


def solution(mesh):
    return jax.shard_map(
        functools.partial(body, mesh.shape["axial"], mesh.shape["radial"]),
        mesh=mesh,
        in_specs=(
            P(None, "axial", "radial", None),
            P(None, "axial", "radial", None),
            P("axial", "radial", None),
            P("axial", "radial", None, None),
            P("axial", "radial"),
            P("axial", "radial", None),
            P("axial", "radial", None, None),
            P("axial", "radial", None),
        ),
        out_specs=(
            P(None, "axial", "radial", None),
            P(None, "axial", "radial", None),
            P("axial", "radial", None, None),
            P("axial", "radial", None, None, None),
        ),
        check_vma=False,
    )
```

```python
import functools

import jax
import jax.numpy as jnp
from jax import lax
from jax.experimental import pallas as pl
from jax.experimental.pallas import tpu as pltpu
from jax.sharding import PartitionSpec as P

MESH = pl.DeviceIdType.MESH
F32, BF16, I32 = jnp.float32, jnp.bfloat16, jnp.int32
time_step = 0.1
CHUNK = 512
TRIPS = (
    ((0, 1), (2, 1, 8, 2), (2, 0)), ((0, 1), (9, 1, 8, 2), (9, 0)), ((0, 1), (3, 6, 8, 2), (3, 0)),
    ((0, -1), (2, 1, 2, 2), (2, 10)), ((0, -1), (9, 1, 2, 2), (9, 10)), ((0, -1), (3, 6, 2, 2), (3, 10)),
    ((1, 0), (8, 2, 2, 8), (0, 2)), ((-1, 0), (2, 2, 2, 8), (10, 2)),
    ((1, 0), (9, 1, 1, 1), (1, 1)), ((-1, 0), (2, 1, 1, 1), (10, 1)),
    ((1, 0), (9, 1, 10, 1), (1, 10)), ((-1, 0), (2, 1, 10, 1), (10, 10)),
)
GROUP = 4
FACES = ((1, 0), (-1, 0), (0, 1), (0, -1))


def coefficient(values, base):
    row = lax.broadcasted_iota(I32, (8, 128), 0)
    kinetic = jnp.where(row >= 5, values * values, 0.0)
    for shift in (4, 2, 1):
        kinetic = kinetic + pltpu.roll(kinetic, shift, 0)
    return base * (1.0 + 0.5 * jnp.tanh(0.5 * kinetic))


def pieces(x):
    high = x.astype(BF16)
    rest = x - high.astype(F32)
    middle = rest.astype(BF16)
    low = (rest - middle.astype(F32)).astype(BF16)
    return high, middle, low


def one_hot(rows, index):
    row = lax.broadcasted_iota(I32, (rows, index.shape[1]), 0)
    return jnp.where(row == index, 1.0, 0.0).astype(BF16)


def dot_nt(a, b):
    return lax.dot_general(a, b, (((1,), (1,)), ((), ())), preferred_element_type=F32)


def z_up(x):
    lane = lax.broadcasted_iota(I32, (8, 128), 1)
    return jnp.where(lane == 127, 0.0, pltpu.roll(x, 127, 1))


class Patch:
    def __init__(self, field, coef, x, column):
        self.field, self.coef, self.x, self.column, self.kept = field, coef, x, column, {}

    def keep(self, key, make):
        if key not in self.kept:
            self.kept[key] = make()
        return self.kept[key]

    def value(self, dx, p):
        return self.keep(("v", dx, p), lambda: self.field[self.x + dx, self.column(p)])

    def own(self, dx, p):
        return self.keep(("c", dx, p), lambda: self.coef[self.x + dx, self.column(p)])

    def flux(self, dx, p, to_x, to_p):
        return self.keep(
            ("f", dx, p, to_x, to_p),
            lambda: (self.own(dx, p) + self.own(to_x, to_p)) * (self.value(to_x, to_p) - self.value(dx, p)),
        )

    def twice_change(self, dx, p):
        lane = lax.broadcasted_iota(I32, (8, 128), 1)
        value, own = self.value(dx, p), self.own(dx, p)
        up = (own + z_up(own)) * (z_up(value) - value)
        down = jnp.where(lane == 0, own * value, pltpu.roll(up, 1, 1))
        flux_x = self.flux(dx, p, dx + 1, p) - self.flux(dx - 1, p, dx, p)
        flux_y = self.flux(dx, p, dx, p + 1) - self.flux(dx, p - 1, dx, p)
        return flux_x + flux_y + (up - down)


def spray_kernel(
    n_a, n_r, species, velocity, diffusivity, parcels, cnt, cells, slots, faces,
    result, staying, arrivals,
    ext, base, start, first, later, source,
    vel, par, cel, slo, fac, vel3, leaving, outgoing,
    load_sem, send_sem, recv_sem, base_send, base_recv, row_send, row_recv,
):
    a, r = lax.axis_index("axial"), lax.axis_index("radial")
    high_late = lax.rem(r, GROUP) >= GROUP // 2
    in_group = lax.rem(r, GROUP)
    inside = jnp.logical_and(in_group != GROUP - 1, jnp.logical_and(lax.rem(a, 2) == 0, a > 0))
    opener = jnp.logical_and(a == 0, r == 0)
    eager = jnp.logical_or(jnp.logical_or(jnp.logical_and(in_group == 0, r > 0), inside), opener)

    def there(step_a, step_r):
        ok = None
        for step, at, size in ((step_a, a, n_a), (step_r, r, n_r)):
            if step:
                here = at < size - 1 if step > 0 else at > 0
                ok = here if ok is None else jnp.logical_and(ok, here)
        return ok

    barrier = pltpu.get_barrier_semaphore()
    total = jnp.int32(0)
    for da, dr in FACES:
        ok = there(da, dr)
        total = total + ok.astype(I32)

        @pl.when(ok)
        def _(da=da, dr=dr):
            pl.semaphore_signal(barrier, inc=1, device_id=(a + da, r + dr), device_id_type=MESH)

    loads = [pltpu.make_async_copy(species.at[f], ext.at[2:10, 2:10, f], load_sem.at[f]) for f in range(5)]
    loads += [pltpu.make_async_copy(velocity.at[k], ext.at[2:10, 2:10, 5 + k], load_sem.at[5 + k]) for k in range(3)]
    loads.append(pltpu.make_async_copy(diffusivity, base.at[2:10, 2:10, 0], load_sem.at[8]))
    own_loads = len(loads)
    for k, (src, dst) in enumerate(
        ((velocity, vel), (parcels, par), (cells, cel), (slots, slo), (faces, fac))
    ):
        loads.append(pltpu.make_async_copy(src, dst, load_sem.at[9 + k]))
    for load in loads:
        load.start()

    zero2 = jnp.zeros((2, 8, 8, 128), F32)
    zero3 = jnp.zeros((8, 2, 8, 128), F32)
    corner = jnp.zeros((8, 128), F32)

    def clear_corner(x, y):
        ext[x, y] = corner
        base[x, y] = corner[:1]

    @pl.when(a == 0)
    def _():
        ext[0:2, 2:10] = zero2
        base[0:2, 2:10] = zero2[:, :, :1]
        arrivals[0] = jnp.zeros((16, 64), F32)
        clear_corner(1, 1)
        clear_corner(1, 10)

    @pl.when(a == n_a - 1)
    def _():
        ext[10:12, 2:10] = zero2
        base[10:12, 2:10] = zero2[:, :, :1]
        arrivals[1] = jnp.zeros((16, 64), F32)
        clear_corner(10, 1)
        clear_corner(10, 10)

    @pl.when(r == 0)
    def _():
        ext[2:10, 0:2] = zero3
        base[2:10, 0:2] = zero3[:, :, :1]
        arrivals[2] = jnp.zeros((16, 64), F32)
        clear_corner(1, 1)
        clear_corner(10, 1)

    @pl.when(r == n_r - 1)
    def _():
        ext[2:10, 10:12] = zero3
        base[2:10, 10:12] = zero3[:, :, :1]
        arrivals[3] = jnp.zeros((16, 64), F32)
        clear_corner(1, 10)
        clear_corner(10, 10)

    source[...] = jnp.zeros((512, 128), F32)

    def gas_at(cell):
        width = cell.shape[1]
        depth_hot = one_hot(128, cell & 127)
        rows = jnp.dot(vel3[...], jnp.concatenate([depth_hot] * 3, axis=0), preferred_element_type=F32)
        here = lax.broadcasted_iota(I32, (64, width), 0) == (cell >> 7)
        gas = [
            jnp.sum(jnp.where(here, rows[64 * k : 64 * k + 64], 0.0), axis=0, keepdims=True) for k in range(3)
        ]
        return jnp.concatenate(gas, axis=0), here, depth_hot

    def push(old, gas):
        drag = old[4:5] * (gas - old[0:3])
        new_velocity = old[0:3] + time_step * drag
        new_mass = old[3:4] * (1.0 - time_step * old[5:6])
        new_position = old[6:9] + time_step * new_velocity
        return drag, jnp.concatenate([new_velocity, new_mass, old[4:6], new_position, old[9:16]], axis=0)

    def find_leavers():
        vel3[...] = jnp.concatenate(pieces(vel[...].reshape(192, 128)), axis=1)
        lane_cells = [cel[:, 128 * h : 128 * h + 128].astype(F32) for h in range(16)]
        stacked = jnp.concatenate([par[:, 128 * h : 128 * h + 128] for h in range(16)] + lane_cells, axis=0)
        stacked3 = jnp.concatenate(pieces(stacked), axis=1)
        leave_sum = jnp.zeros((16, 128), F32)
        moved, moved_cells = [], []
        for f in range(4):
            member = lax.broadcasted_iota(I32, (1, 64), 1)
            slot = jnp.where(member < fac[0:1, f : f + 1], slo[f : f + 1, :], -1)
            high, low_hot = slot >> 7, one_hot(128, slot & 127)
            leave_sum = leave_sum + dot_nt(one_hot(16, high), low_hot)
            picked = jnp.dot(stacked3, jnp.concatenate([low_hot] * 3, axis=0), preferred_element_type=F32)
            out = jnp.zeros((16, 64), F32)
            for h in range(16):
                out = out + jnp.where(high == h, picked[16 * h : 16 * h + 16], 0.0)
            chosen = lax.broadcasted_iota(I32, (16, 64), 0) == high
            moved.append(out)
            moved_cells.append(jnp.sum(jnp.where(chosen, picked[256:272], 0.0), axis=0, keepdims=True))
        leaving[...] = leave_sum

        for f in range(4):
            gas, _, _ = gas_at(moved_cells[f].astype(I32))
            member = lax.broadcasted_iota(I32, (1, 64), 1)
            outgoing[f] = jnp.where(member < fac[0:1, f : f + 1], push(moved[f], gas)[1], 0.0)

    def parcel_step(c, _):
        span = pl.ds(pl.multiple_of(c * CHUNK, CHUNK), CHUNK)
        gas, here, depth_hot = gas_at(cel[:, span])
        old = par[:, span]
        mass, evaporation = old[3:4], old[5:6]
        drag, new = push(old, gas)
        live = lax.broadcasted_iota(I32, (1, CHUNK), 1) + c * CHUNK < cnt[0, 0]
        leave = jnp.concatenate(
            [leaving[pl.ds(c * (CHUNK // 128) + j, 1), :] for j in range(CHUNK // 128)], axis=1
        )
        staying[:, span] = jnp.where(jnp.logical_and(live, leave == 0.0), new, 0.0)
        deposit = [mass * evaporation] + [-mass * drag[k : k + 1] for k in range(3)]
        split = [pieces(jnp.where(live, d, 0.0)) for d in deposit]
        added = jnp.zeros((256, 128), F32)
        for p in range(3):
            spread = jnp.concatenate(
                [jnp.where(here, split[k][p].astype(F32), 0.0).astype(BF16) for k in range(4)], axis=0
            )
            added = added + dot_nt(spread, depth_hot)
        source[0:64] += added[0:64]
        source[320:512] += added[64:256]
        return 0

    for load in loads:
        load.wait()

    chunks = 2048 // CHUNK
    ahead = jnp.where(eager, 0, chunks)
    pl.when(jnp.logical_not(eager))(find_leavers)
    lax.fori_loop(0, ahead, parcel_step, 0)

    pl.semaphore_wait(barrier, total)

    def trip(k):
        (da, dr), (sx, nx, sy, ny), (tx, ty) = TRIPS[k]
        device = (a + da, r + dr)
        return (
            pltpu.make_async_remote_copy(
                src_ref=ext.at[sx : sx + nx, sy : sy + ny],
                dst_ref=ext.at[tx : tx + nx, ty : ty + ny],
                send_sem=send_sem.at[k], recv_sem=recv_sem.at[k],
                device_id=device, device_id_type=MESH,
            ),
            pltpu.make_async_remote_copy(
                src_ref=base.at[sx : sx + nx, sy : sy + ny],
                dst_ref=base.at[tx : tx + nx, ty : ty + ny],
                send_sem=base_send.at[k], recv_sem=base_recv.at[k],
                device_id=device, device_id_type=MESH,
            ),
        )

    def sends(k):
        da, dr = TRIPS[k][0]
        out, back = there(da, dr), there(-da, -dr)
        if k >= 8:
            side = there(0, -1) if k < 10 else there(0, 1)
            out, back = jnp.logical_and(out, side), jnp.logical_and(back, side)
        return out, back

    def send(trips, ok=None):
        for k in trips:
            out, _ = sends(k)

            @pl.when(out if ok is None else jnp.logical_and(out, ok))
            def _(k=k):
                for copy in trip(k):
                    copy.start()

    def receive(trips, ok=None):
        for k in trips:
            _, back = sends(k)

            @pl.when(back if ok is None else jnp.logical_and(back, ok))
            def _(k=k):
                for copy in trip(k):
                    copy.wait_recv()

    to_high, to_low = lax.rem(r, GROUP) == GROUP - 1, lax.rem(r, GROUP) == 0
    send((0, 1), to_high)
    send((3, 4), to_low)
    even = lax.rem(a, 2) == 0
    send((5,), jnp.logical_and(to_low, even))
    send((6, 7))
    send((2,), jnp.logical_and(to_high, even))
    send((0, 1, 2), jnp.logical_not(to_high))
    send((3, 4, 5), jnp.logical_not(to_low))

    def row_copy(f):
        da, dr = FACES[f]
        return pltpu.make_async_remote_copy(
            src_ref=outgoing.at[f], dst_ref=arrivals.at[f],
            send_sem=row_send.at[f], recv_sem=row_recv.at[f],
            device_id=(a + da, r + dr), device_id_type=MESH,
        )

    def send_rows(ok):
        for f in (2, 3, 0, 1):

            @pl.when(jnp.logical_and(there(*FACES[f]), ok))
            def _(f=f):
                row_copy(f).start()

    send_rows(jnp.logical_not(eager))

    pl.when(eager)(find_leavers)

    def own_start(x, _):
        for y in range(2, 10):
            start[x, y] = coefficient(ext[x, y], base[x, y])
        return 0

    lax.fori_loop(2, 10, own_start, 0)
    send_rows(eager)
    send((2,), jnp.logical_and(to_high, jnp.logical_not(even)))
    send((5,), jnp.logical_and(to_low, jnp.logical_not(even)))
    low_late = jnp.logical_not(high_late)

    def hand_on(ok, early):
        for is_high in (False, True):
            chosen = jnp.logical_and(ok, low_late if is_high == early else high_late)
            receive((3, 4) if is_high else (0, 1), chosen)
            send((10, 11) if is_high else (8, 9), chosen)

    hand_on(eager, True)
    lax.fori_loop(ahead, chunks, parcel_step, 0)

    def find_start(x, y):
        start[x, y] = coefficient(ext[x, y], base[x, y])

    def find_first(patch, dx, p, outside):
        x, y = patch.x + dx, patch.column(p)
        new = patch.value(dx, p) + (0.5 * time_step) * patch.twice_change(dx, p)
        if outside is not None:
            new = jnp.where(outside, 0.0, new)
        first[x, y] = new
        later[x, y] = coefficient(new, base[x, y])

    def find_second(patch, dx, p):
        x, y = patch.x + dx, patch.column(p)
        cell = (x - 2) * 8 + (y - 2)
        result[pl.ds(cell, 8, stride=64), :] = (
            0.5 * (ext[x, y] + patch.value(dx, p))
            + (0.25 * time_step) * patch.twice_change(dx, p)
            + time_step * source[pl.ds(cell, 8, stride=64), :]
        )

    def repeat(low, high, step):
        def run(i, _):
            step(i)
            return 0

        lax.fori_loop(low, high, run, 0)

    def inner_first(x):
        patch = Patch(ext, start, x, lambda p: p)
        for p in range(3, 9):
            find_first(patch, 0, p, None)

    def inner_second(x):
        patch = Patch(first, later, x, lambda p: p)
        for p in range(4, 8):
            find_second(patch, 0, p)

    repeat(3, 9, inner_first)
    repeat(4, 8, inner_second)
    hand_on(jnp.logical_not(eager), True)
    hand_on(jnp.logical_not(even), False)

    places = [jnp.where(high_late, p, 11 - p) for p in range(12)]

    def column(p):
        return places[p]

    early_edge = jnp.where(high_late, r == 0, r == n_r - 1)
    late_edge = jnp.where(high_late, r == n_r - 1, r == 0)

    receive((6, 7))
    receive((2, 8, 9), high_late)
    receive((5, 10, 11), low_late)

    def early_side_start(i):
        for dx in range(4):
            for p in (0, 1):
                find_start(2 + 4 * i + dx, column(p))

    def early_end_start(i):
        for p in range(2, 10):
            find_start(11 * i, column(p))
        for p in range(1, 10):
            find_start(1 + 9 * i, column(p))

    repeat(0, 2, early_side_start)
    repeat(0, 2, early_end_start)

    def early_end_first(i):
        outer = Patch(ext, start, 1 + 9 * i, column)
        for p in range(2, 9):
            find_first(outer, 0, p, jnp.where(i == 0, a == 0, a == n_a - 1))
        inner = Patch(ext, start, 2 + 7 * i, column)
        for p in range(1, 9):
            find_first(inner, 0, p, early_edge if p == 1 else None)

    def early_side_first(i):
        patch = Patch(ext, start, 3 + 3 * i, column)
        for dx in range(3):
            find_first(patch, dx, 1, early_edge)
            find_first(patch, dx, 2, None)

    repeat(0, 2, early_end_first)
    repeat(0, 2, early_side_first)

    def early_end_second(i):
        patch = Patch(first, later, 2 + 6 * i, column)
        for dx in (0, 1):
            for p in range(2, 8):
                find_second(patch, dx, p)

    def early_side_second(i):
        patch = Patch(first, later, 4 + 2 * i, column)
        for dx in (0, 1):
            for p in (2, 3):
                find_second(patch, dx, p)

    repeat(0, 2, early_end_second)
    repeat(0, 2, early_side_second)

    hand_on(even, False)
    receive((5, 10, 11), high_late)
    receive((2, 8, 9), low_late)

    for x in range(2, 10):
        for p in (10, 11):
            find_start(x, column(p))
    for x in (1, 10):
        find_start(x, column(10))
    patch = Patch(ext, start, 0, column)
    find_first(patch, 1, 9, a == 0)
    for x in range(2, 10):
        find_first(patch, x, 9, None)
        find_first(patch, x, 10, late_edge)
    find_first(patch, 10, 9, a == n_a - 1)
    patch = Patch(first, later, 0, column)
    for x in range(2, 10):
        for p in (8, 9):
            find_second(patch, x, p)

    for f, (da, dr) in enumerate(FACES):

        @pl.when(there(-da, -dr))
        def _(f=f):
            row_copy(f).wait_recv()

    for k in range(12):

        @pl.when(sends(k)[0])
        def _(k=k):
            for copy in trip(k):
                copy.wait_send()

    for f, (da, dr) in enumerate(FACES):

        @pl.when(there(da, dr))
        def _(f=f):
            row_copy(f).wait_send()


def store_kernel(result, staying, arrivals, species_out, velocity_out, staying_out, arrivals_out, sems):
    copies = [
        pltpu.make_async_copy(src, dst, sems.at[k])
        for k, (src, dst) in enumerate(
            (
                (result.at[0:320], species_out), (result.at[320:512], velocity_out),
                (staying, staying_out), (arrivals, arrivals_out),
            )
        )
    ]
    for copy in copies:
        copy.start()
    for copy in copies:
        copy.wait()


def body(n_a, n_r, species, velocity, diffusivity, parcels, counts, cells, leave_slots, leave_counts):
    anywhere = pl.BlockSpec(memory_space=pl.ANY)
    vmem = pl.BlockSpec(memory_space=pltpu.VMEM)
    shape = lambda *dims: jax.ShapeDtypeStruct(dims, F32)
    local = lambda *dims: pltpu.VMEM(dims, F32)
    dma = pltpu.SemaphoreType.DMA
    between = pl.pallas_call(
        functools.partial(spray_kernel, n_a, n_r),
        name="spray",
        out_shape=[local(512, 128), local(16, 2048), local(4, 16, 64)],
        in_specs=[anywhere] * 4 + [pl.BlockSpec(memory_space=pltpu.SMEM)] + [anywhere] * 3,
        out_specs=[vmem] * 3,
        scratch_shapes=[
            local(12, 12, 8, 128), local(12, 12, 1, 128), local(12, 12, 8, 128), local(12, 12, 8, 128),
            local(12, 12, 8, 128), local(512, 128),
            local(3, 8, 8, 128), local(16, 2048),
            pltpu.VMEM((1, 2048), I32), pltpu.VMEM((4, 64), I32), pltpu.VMEM((1, 4), I32),
            pltpu.VMEM((192, 384), BF16), local(16, 128), local(4, 16, 64),
            dma((14,)), dma((12,)), dma((12,)), dma((12,)), dma((12,)), dma((4,)), dma((4,)),
        ],
        compiler_params=pltpu.CompilerParams(collective_id=0, has_side_effects=True),
    )(
        species, velocity, diffusivity, parcels[0, 0], counts, cells[0], leave_slots[0, 0], leave_counts[0],
    )
    species_out, velocity_out, staying, arrivals = pl.pallas_call(
        store_kernel,
        name="store",
        out_shape=[shape(320, 128), shape(192, 128), shape(16, 2048), shape(4, 16, 64)],
        in_specs=[vmem] * 3,
        out_specs=[anywhere] * 4,
        scratch_shapes=[dma((4,))],
    )(*[pltpu.with_memory_space_constraint(x, pltpu.VMEM) for x in between])
    return (
        species_out.reshape(5, 8, 8, 128), velocity_out.reshape(3, 8, 8, 128),
        staying[None, None], arrivals[None, None],
    )


def solution(mesh):
    return jax.shard_map(
        functools.partial(body, mesh.shape["axial"], mesh.shape["radial"]),
        mesh=mesh,
        in_specs=(
            P(None, "axial", "radial", None),
            P(None, "axial", "radial", None),
            P("axial", "radial", None),
            P("axial", "radial", None, None),
            P("axial", "radial"),
            P("axial", "radial", None),
            P("axial", "radial", None, None),
            P("axial", "radial", None),
        ),
        out_specs=(
            P(None, "axial", "radial", None),
            P(None, "axial", "radial", None),
            P("axial", "radial", None, None),
            P("axial", "radial", None, None, None),
        ),
        check_vma=False,
    )
```
